32 devices in a mesh: pole: 2 (over y), row: 8 (over z, x), col: 2 (over core).
Axes of the slice: x: 2, y: 2, z: 4, core: 2. Of those that a mesh axis runs over, the one named last changes fastest.
Arguments:
- known_inverse: float32 [16, 128, 1024], P('pole', 'col', 'row'), parts along dimension 0, may hold values from -1 to 3, as said below
- first_factor: float32 [2048, 512], P(('pole', 'row')), parts along dimension 0, may hold values from -0.5 to 0.5
- first_corner: float32 [1024, 512], P('pole'), parts along dimension 0, may hold values from -1 to 5, as said below
- first_ancestors: int32 [1024], P('pole'), parts along dimension 0, may hold values from 0 to 1023, as said below
- second_factor: float32 [2048, 512], P(('pole', 'row')), parts along dimension 0, may hold values from -0.75 to 0.75
- second_link: float32 [1024, 512], P('pole'), parts along dimension 0, may hold values from -0.25 to 0.25
- second_corner: float32 [1024, 512], P('pole', 'col'), parts along dimension 0, may hold values from -1 to 5, as said below
- second_ancestors: int32 [512], P('pole'), parts along dimension 0, may hold values from 0 to 1023, as said below
Outputs:
- first_column: float32 [2048, 512], P(('pole', 'row'), 'col'), parts along dimension 0
- first_diagonal: float32 [1024, 512], P('pole', 'col'), parts along dimension 0
- second_column: float32 [2048, 512], P(('pole', 'row'), 'col'), parts along dimension 0
- second_cross: float32 [1024, 512], P('pole', 'col'), parts along dimension 0
- second_diagonal: float32 [1024, 512], P('pole', 'col'), parts along dimension 0
The draws below stay inside these ranges and needn't reach their ends.
There are 2 independent parts, one for each index of `pole`. The reference program is written for one: setup_inputs(seed, part) draws one part's arguments, and reference() takes and returns one part's arrays. A program takes and returns all parts, laid end to end along the dimension named above; each array names one. Nothing has to cross between parts.
Inputs may be any that keep to these rules, and one draw needn't show every extreme that they name: `known_inverse`: K is symmetric. `first_corner`: symmetric. `second_corner`: symmetric. `first_ancestors`: distinct row numbers; every block of 128 consecutive row numbers starting at a multiple of 128 holds at least one of them. `second_ancestors`: distinct row numbers, each of which is also in first_ancestors; every block of 128 consecutive row numbers starting at a multiple of 128 holds at least one of them.
All inputs are finite; a program needn't handle non-finite values.
Results may differ from the reference program's by a relative error of at most 0.000084.
Values sent between devices are 32-bit elements; how exact they have to be, the bound alone decides.
No kernel may reach another device: no remote copies, remote signals or barrier semaphores. Data moves between devices by JAX's collectives and lax.ppermute only.
A program may use at most 128 MiB of HBM per device.

```python
import jax
import jax.numpy as jnp
from jax import lax

BLOCK_ROWS = 128
WIDTH = 512
ANC_ROWS = 1024
FIRST_ANC = 512
SECOND_ANC = 256
N_ROW = 8


def symmetric_draw(key, order, lowest, highest, spread):
    noise_key, middle_key = jax.random.split(key)
    noise = jnp.clip(jax.random.normal(noise_key, (order, order), jnp.float32), -4.0, 4.0) * (spread / order ** 0.5)
    middle = jax.random.uniform(middle_key, (order,), jnp.float32, lowest, highest)
    return (noise + noise.T) * 0.5 + jnp.diag(middle)


def draw_known_inverse(key, part):
    whole = symmetric_draw(jax.random.fold_in(key, 3), ANC_ROWS, 0.5, 2.0, 0.5)
    return whole.reshape(N_ROW, BLOCK_ROWS, ANC_ROWS)


def draw_first_corner(key, part):
    return symmetric_draw(jax.random.fold_in(key, 5), WIDTH, 1.0, 3.0, 0.5)


def draw_second_corner(key, part):
    return symmetric_draw(jax.random.fold_in(key, 7), WIDTH, 1.0, 3.0, 0.5)


def ancestor_sets(key):
    numbers = jnp.arange(ANC_ROWS, dtype=jnp.int32)
    places = jax.random.randint(jax.random.fold_in(key, 20), (N_ROW,), 0, BLOCK_ROWS, dtype=jnp.int32)
    keeper = (numbers % BLOCK_ROWS == places[numbers // BLOCK_ROWS]).astype(jnp.int32)
    scores = keeper * ANC_ROWS + jax.random.randint(jax.random.fold_in(key, 21), (ANC_ROWS,), 0, ANC_ROWS, dtype=jnp.int32)
    chosen = jnp.sort(lax.top_k(scores * ANC_ROWS + numbers, FIRST_ANC)[1]).astype(jnp.int32)
    inner = jnp.arange(FIRST_ANC, dtype=jnp.int32)
    inner_scores = keeper[chosen] * ANC_ROWS + jax.random.randint(jax.random.fold_in(key, 22), (FIRST_ANC,), 0, ANC_ROWS, dtype=jnp.int32)
    subset = jnp.sort(chosen[lax.top_k(inner_scores * FIRST_ANC + inner, SECOND_ANC)[1]]).astype(jnp.int32)
    return (chosen, subset)


def draw_first_ancestors(key, part):
    return ancestor_sets(key)[0]


def draw_second_ancestors(key, part):
    return ancestor_sets(key)[1]


def levels(own_key, shape, pieces, least, high):
    gain, own = 1.0, jax.random.fold_in(own_key, 6)
    for axis_at, parts in pieces:
        draws = jnp.exp(jax.random.uniform(jax.random.fold_in(own, axis_at), (parts,), jnp.float32, least / len(pieces), high / len(pieces)))
        gain = gain * jnp.repeat(draws, shape[axis_at] // parts).reshape([-1 if axis == axis_at else 1 for axis in range(len(shape))])
    return gain


def bell_draw(own_key, extent, scale, most, shards=(), kind=jnp.bfloat16):
    array = scale * jax.random.normal(own_key, extent, jnp.float32)
    if shards:
        array = array * levels(own_key, extent, shards, -0.22, 0.18)
    return jnp.clip(array, -most, most).astype(kind)


def setup_inputs(seed: int = 0, part: int = 0) -> dict:
    key_of = jax.random.split(jax.random.key(seed), 9)
    part_keys = jax.random.split(jax.random.fold_in(key_of[8], part), 9)
    known_inverse = draw_known_inverse(jax.random.fold_in(jax.random.fold_in(key_of[8], part), 71), part)
    first_factor = bell_draw(part_keys[1], (ANC_ROWS, WIDTH), (FIRST_ANC // 4) ** -0.5, 0.5, ((0, 8),), jnp.float32)
    first_corner = draw_first_corner(jax.random.fold_in(jax.random.fold_in(key_of[8], part), 71), part)
    first_ancestors = draw_first_ancestors(jax.random.fold_in(jax.random.fold_in(key_of[8], part), 71), part)
    second_factor = bell_draw(part_keys[4], (ANC_ROWS, WIDTH), (SECOND_ANC // 4) ** -0.5, 0.75, ((0, 8),), jnp.float32)
    second_link = bell_draw(part_keys[5], (WIDTH, WIDTH), WIDTH ** -0.5, 0.25, (), jnp.float32)
    second_corner = draw_second_corner(jax.random.fold_in(jax.random.fold_in(key_of[8], part), 71), part)
    second_ancestors = draw_second_ancestors(jax.random.fold_in(jax.random.fold_in(key_of[8], part), 71), part)
    return {"known_inverse": known_inverse, "first_factor": first_factor, "first_corner": first_corner, "first_ancestors": first_ancestors, "second_factor": second_factor, "second_link": second_link, "second_corner": second_corner, "second_ancestors": second_ancestors}


HIGH = lax.Precision.HIGHEST


def product(left, right):
    return jnp.dot(left, right, precision=HIGH, preferred_element_type=jnp.float32)


def transposed_product(left, right):
    return lax.dot_general(left, right, (((0,), (0,)), ((), ())), precision=HIGH, preferred_element_type=jnp.float32)


def row_mask(ancestors):
    return jnp.zeros((ANC_ROWS,), jnp.float32).at[ancestors].set(1.0)[:, None]


def reference(known_inverse, first_factor, first_corner, first_ancestors, second_factor, second_link, second_corner, second_ancestors):
    columns = known_inverse.reshape(ANC_ROWS, ANC_ROWS)
    first_mask = row_mask(first_ancestors)
    second_mask = row_mask(second_ancestors)
    first_masked = first_factor * first_mask
    second_masked = second_factor * second_mask
    first_column = -(transposed_product(columns, first_masked) * first_mask)
    first_diagonal = first_corner - transposed_product(first_masked, first_column)
    second_column = -((transposed_product(columns, second_masked) + product(first_column, second_link)) * second_mask)
    second_cross = -(transposed_product(first_column, second_masked) + product(first_diagonal, second_link))
    second_diagonal = second_corner - transposed_product(second_masked, second_column) - transposed_product(second_link, second_cross)
    return (first_column, first_diagonal, second_column, second_cross, second_diagonal)
```

```python
import functools

import jax
import jax.numpy as jnp
from jax import lax
from jax.experimental import pallas as pl
from jax.experimental.pallas import tpu as pltpu
from jax.sharding import PartitionSpec as P

HIGH = lax.Precision.HIGHEST
F32, BF16 = jnp.float32, jnp.bfloat16
NN = (((1,), (0,)), ((), ()))
NT = (((1,), (1,)), ((), ()))
TN = (((0,), (0,)), ((), ()))
VMEM = pl.BlockSpec(memory_space=pltpu.VMEM)
SMEM = pl.BlockSpec(memory_space=pltpu.SMEM)
ANY = pl.BlockSpec(memory_space=pl.ANY)


def product(left, right):
    return jnp.dot(left, right, precision=HIGH, preferred_element_type=F32)


def transposed_product(left, right):
    return lax.dot_general(left, right, TN, precision=HIGH, preferred_element_type=F32)


def mask_of(ancestors, row_start, rows):
    numbers = row_start + jnp.arange(rows, dtype=jnp.int32)
    return jnp.any(ancestors[:, None] == numbers[None, :], axis=0).astype(F32)


def reduce_plan(known_inverse, first_factor, first_corner, first_ancestors, second_factor, second_link, second_corner, second_ancestors):
    groups, share_rows, block_rows = known_inverse.shape
    half_width = second_corner.shape[1]
    col_index = lax.axis_index("col")
    row_start = lax.axis_index("row") * block_rows
    first_mask = mask_of(first_ancestors, row_start, block_rows)[:, None]
    second_mask = mask_of(second_ancestors, row_start, block_rows)[:, None]
    first_masked = first_factor * first_mask
    second_masked = second_factor * second_mask
    share_start = col_index * share_rows
    first_piece = lax.dynamic_slice_in_dim(first_masked, share_start, share_rows, 0)
    second_piece = lax.dynamic_slice_in_dim(second_masked, share_start, share_rows, 0)
    columns = known_inverse.reshape(groups * share_rows, block_rows)
    first_partial = transposed_product(columns, lax.all_gather(first_piece, "row", axis=0, tiled=True))
    second_partial = transposed_product(columns, lax.all_gather(second_piece, "row", axis=0, tiled=True))
    first_image = lax.psum_scatter(first_partial, "col", scatter_dimension=1, tiled=True)
    first_column = -(first_image * first_mask)
    first_full = lax.all_gather(first_column, "col", axis=1, tiled=True)
    diagonal_partial = transposed_product(first_masked, first_column)
    corner_half = lax.dynamic_slice_in_dim(first_corner, col_index * half_width, half_width, 1)
    first_diagonal = corner_half - lax.psum(diagonal_partial, "row")
    diagonal_full = lax.all_gather(first_diagonal, "col", axis=1, tiled=True)
    second_image = lax.psum_scatter(second_partial, "col", scatter_dimension=1, tiled=True)
    link_half = lax.dynamic_slice_in_dim(second_link, col_index * half_width, half_width, 1)
    second_column = -((second_image + product(first_full, link_half)) * second_mask)
    second_half = lax.dynamic_slice_in_dim(second_masked, col_index * half_width, half_width, 1)
    cross_partial = transposed_product(first_full, second_half)
    closing_partial = transposed_product(second_masked, second_column)
    cross_total, closing_total = lax.psum((cross_partial, closing_partial), "row")
    second_cross = -(cross_total + product(diagonal_full, link_half))
    second_diagonal = second_corner - closing_total - transposed_product(second_link, second_cross)
    return (first_column, first_diagonal, second_column, second_cross, second_diagonal)


def dot(left, right, dims):
    return lax.dot_general(left, right, dims, preferred_element_type=F32)


def split(value):
    high = value.astype(BF16)
    return high, (value - high.astype(F32)).astype(BF16)


def dot3(left, right, dims):
    (lh, ll), (rh, rl) = left, right
    return dot(lh, rh, dims) + (dot(lh, rl, dims) + dot(ll, rh, dims))


def dot2(exact, right, dims, flip=False):
    rh, rl = right
    if flip:
        return dot(rh, exact, dims) + dot(rl, exact, dims)
    return dot(exact, rh, dims) + dot(exact, rl, dims)


def slot_codes(mask):
    block = mask.shape[1]
    before = (lax.broadcasted_iota(jnp.int32, (block, block), 0) < lax.broadcasted_iota(jnp.int32, (block, block), 1)).astype(BF16)
    rank = dot(mask.astype(BF16), before, NN)
    return jnp.where(mask > 0, rank, -1.0).astype(jnp.int32)


def picker(code_row, slots, offset=0):
    block = code_row.shape[1]
    at = lax.broadcasted_iota(jnp.int32, (slots, block), 0) - offset
    return ((at == code_row) & (code_row >= 0)).astype(BF16)


def prepare_kernel(cap, place, mask1, mask2, first, second, link, mine, theirs, out, code, m2, cols):
    row, col = place[0], place[1]
    groups, share, block = mine.shape
    width = first.shape[1]
    code[...] = slot_codes(mask1[...])
    m2[...] = mask2[...]
    pick = picker(code[pl.ds(row, 1), :], cap)
    pick2 = (pick.astype(F32) * m2[pl.ds(row, 1), :]).astype(BF16)
    first_c = dot2(pick, split(first[...]), NN)
    second_c = dot2(pick2, split(second[...]), NN)
    out[:, :width] = first_c
    out[:, width : 2 * width] = second_c - dot3(split(first_c), split(link[...]), NN)
    for g in range(groups):
        base = g * block
        cols[pl.ds(pl.multiple_of(base + col * share, share), share), :] = mine[g]
        cols[pl.ds(pl.multiple_of(base + (1 - col) * share, share), share), :] = theirs[g]
    half = dot2(pick, split(cols[...]), NT)
    wide = out.shape[1] - 2 * width
    total = jnp.zeros((cap, wide), F32)
    for g in range(groups):
        spread = picker(code[g : g + 1, :], wide, g * cap)
        total += dot2(spread, split(half[:, g * block : (g + 1) * block]), NT, flip=True)
    out[:, 2 * width :] = total


def finish_kernel(cap, sources, *refs):
    place, mask1, mask2 = refs[:3]
    own = refs[3]
    n = len(sources)
    near, far = refs[4 : 4 + n], refs[4 + n : 4 + 2 * n]
    corner1, corner2, cross0, diag0 = refs[4 + 2 * n : 8 + 2 * n]
    outs = refs[8 + 2 * n : 13 + 2 * n]
    ft, known, code, m2, c1, g1, c2, xx, g2, sems = refs[13 + 2 * n :]
    row, col = place[0], place[1]
    width = own.shape[1] - known.shape[1]
    width //= 2
    half_width = width // 2
    half = cap // 2

    code[...] = slot_codes(mask1[...])
    m2[...] = mask2[...]

    def put(value, start, rows):
        at = pl.ds(pl.multiple_of(start, 8), rows)
        ft[at, :] = value[:, : 2 * width]
        known[at, :] = value[:, 2 * width :]

    put(own[...], row * cap, cap)
    for source, a, b in zip(sources, near, far):
        base = source(row) * cap
        put(a[...], base + col * half, half)
        put(b[...], base + (1 - col) * half, half)

    start = pl.multiple_of(col * half_width, half_width)
    right_f = split(ft[:, pl.ds(start, half_width)])
    right_t = split(ft[:, pl.ds(pl.multiple_of(width + start, half_width), half_width)])
    k = split(known[...])
    image_f = dot3(k, right_f, NN)
    image_t = dot3(k, right_t, NN)
    c1[...] = image_f
    c2[...] = image_t
    mine = pl.ds(pl.multiple_of(row * cap, 8), cap)
    own_f, own_t = split(c1[mine, :]), split(c2[mine, :])
    pick = picker(code[pl.ds(row, 1), :], cap)
    pick2 = (pick.astype(F32) * m2[pl.ds(row, 1), :]).astype(BF16)
    block = code.shape[1]
    c1[:block, :] = -dot2(pick, own_f, TN)
    c2[:block, :] = -dot2(pick2, own_t, TN)
    copies = [
        pltpu.make_async_copy(c1.at[:block], outs[0], sems.at[0]),
        pltpu.make_async_copy(c2.at[:block], outs[2], sems.at[2]),
    ]
    for copy in copies:
        copy.start()
    image_f, image_t = split(image_f), split(image_t)
    left_f = split(ft[:, :width])
    left_t = split(ft[:, width:])
    g1[...] = corner1[...] + dot3(left_f, image_f, TN)
    copies.append(pltpu.make_async_copy(g1, outs[1], sems.at[1]))
    copies[-1].start()
    xx[...] = dot3(left_f, image_t, TN) - cross0[...]
    copies.append(pltpu.make_async_copy(xx, outs[3], sems.at[3]))
    copies[-1].start()
    g2[...] = corner2[...] + (diag0[...] + dot3(left_t, image_t, TN))
    copies.append(pltpu.make_async_copy(g2, outs[4], sems.at[4]))
    copies[-1].start()
    for copy in copies:
        copy.wait()


def gather_branch(cap, n, place, mask1, mask2, known_inverse, theirs, first_factor, second_factor, second_link, corner1, second_corner, cross0, diag0):
    groups, share, block = known_inverse.shape
    width = first_factor.shape[1]
    half_width = second_corner.shape[1]
    wide = -(-n * cap // 128) * 128
    cost = pl.CostEstimate(flops=2 * cap * width * (width + n * block), bytes_accessed=4 * width * width * 2, transcendentals=0)
    payload = pl.pallas_call(
        functools.partial(prepare_kernel, cap),
        out_shape=jax.ShapeDtypeStruct((cap, 2 * width + wide), F32),
        in_specs=[SMEM] + [VMEM] * 7,
        out_specs=VMEM,
        scratch_shapes=[
            pltpu.VMEM((n, block), jnp.int32),
            pltpu.VMEM((n, block), F32),
            pltpu.VMEM((n * block, block), F32),
        ],
        cost_estimate=cost,
        name="prepare",
    )(place, mask1, mask2, first_factor, second_factor, second_link, known_inverse, theirs)

    half = cap // 2
    ring = [(r, (r + 2) % n) for r in range(n)]
    pair = [(r, r ^ 1) for r in range(n)]
    swap = [(0, 1), (1, 0)]
    own_half = lax.dynamic_slice_in_dim(payload, lax.axis_index("col") * half, half, 0)
    along = [own_half]
    sources, near = [], []
    across = [lax.ppermute(own_half, "row", pair)]
    for step in range(1, n // 2):
        along.append(lax.ppermute(along[-1], "row", ring))
        across.append(lax.ppermute(along[-1], "row", pair))
    for step in range(n // 2):
        if step:
            near.append(along[step])
            sources.append(lambda r, s=step: lax.rem(r - 2 * s + n, n))
        near.append(across[step])
        sources.append(lambda r, s=step: lax.rem(lax.rem(r, 2) * -2 + 1 + r - 2 * s + n, n))
    far = [lax.ppermute(v, "col", swap) for v in near]

    rows = wide
    outs = (
        jax.ShapeDtypeStruct((block, half_width), F32),
        jax.ShapeDtypeStruct((width, half_width), F32),
        jax.ShapeDtypeStruct((block, half_width), F32),
        jax.ShapeDtypeStruct((width, half_width), F32),
        jax.ShapeDtypeStruct((width, half_width), F32),
    )
    m = len(near)
    cost = pl.CostEstimate(flops=2 * 3 * (rows * rows * width + 3 * width * rows * half_width), bytes_accessed=4 * rows * (2 * width + wide), transcendentals=0)
    return pl.pallas_call(
        functools.partial(finish_kernel, cap, sources),
        out_shape=outs,
        in_specs=[SMEM] + [VMEM] * (7 + 2 * m),
        out_specs=[ANY] * 5,
        scratch_shapes=[
            pltpu.VMEM((rows, 2 * width), F32),
            pltpu.VMEM((rows, wide), F32),
            pltpu.VMEM((n, block), jnp.int32),
            pltpu.VMEM((n, block), F32),
            pltpu.VMEM((max(rows, block), half_width), F32),
            pltpu.VMEM((width, half_width), F32),
            pltpu.VMEM((max(rows, block), half_width), F32),
            pltpu.VMEM((width, half_width), F32),
            pltpu.VMEM((width, half_width), F32),
            pltpu.SemaphoreType.DMA((5,)),
        ],
        compiler_params=pltpu.CompilerParams(vmem_limit_bytes=48 << 20),
        cost_estimate=cost,
        name="finish",
    )(place, mask1, mask2, payload, *near, *far, corner1, second_corner, cross0, diag0)


def gather_plan(n, known_inverse, first_factor, first_corner, first_ancestors, second_factor, second_link, second_corner, second_ancestors):
    groups, share, block = known_inverse.shape
    half_width = second_corner.shape[1]
    row, col = lax.axis_index("row"), lax.axis_index("col")
    place = jnp.stack([row, col]).astype(jnp.int32)
    theirs = lax.ppermute(known_inverse, "col", [(0, 1), (1, 0)])
    mask1 = mask_of(first_ancestors, 0, n * block).reshape(n, block)
    mask2 = mask_of(second_ancestors, 0, n * block).reshape(n, block)
    start = col * half_width
    corner1 = lax.dynamic_slice_in_dim(first_corner, start, half_width, 1)
    link_half = lax.dynamic_slice_in_dim(second_link, start, half_width, 1)
    cross0 = product(first_corner, link_half)
    diag0 = transposed_product(second_link, cross0)
    return gather_branch(block, n, place, mask1, mask2, known_inverse, theirs, first_factor, second_factor, second_link, corner1, second_corner, cross0, diag0)


def solution(mesh):
    n = mesh.shape["row"]

    def on_device(known_inverse, *rest):
        groups, share, block = known_inverse.shape
        width = rest[0].shape[1]
        if n % 2 == 0 and mesh.shape["col"] == 2 and (n * block) ** 2 <= 12 * width**2:
            return gather_plan(n, known_inverse, *rest)
        return reduce_plan(known_inverse, *rest)

    return jax.shard_map(
        on_device,
        mesh=mesh,
        in_specs=(
            P("pole", "col", "row"),
            P(("pole", "row"), None),
            P("pole", None),
            P("pole"),
            P(("pole", "row"), None),
            P("pole", None),
            P("pole", "col"),
            P("pole"),
        ),
        out_specs=(
            P(("pole", "row"), "col"),
            P("pole", "col"),
            P(("pole", "row"), "col"),
            P("pole", "col"),
            P("pole", "col"),
        ),
        check_vma=False,
    )
```

```python
import functools

import jax
import jax.numpy as jnp
from jax import lax
from jax.experimental import pallas as pl
from jax.experimental.pallas import tpu as pltpu
from jax.sharding import PartitionSpec as P


HIGH = lax.Precision.HIGHEST
F32, BF16 = jnp.float32, jnp.bfloat16
NN = (((1,), (0,)), ((), ()))
NT = (((1,), (1,)), ((), ()))
TN = (((0,), (0,)), ((), ()))
VMEM = pl.BlockSpec(memory_space=pltpu.VMEM)
SMEM = pl.BlockSpec(memory_space=pltpu.SMEM)
ANY = pl.BlockSpec(memory_space=pl.ANY)


def product(left, right):
    return jnp.dot(left, right, precision=HIGH, preferred_element_type=F32)


def transposed_product(left, right):
    return lax.dot_general(left, right, TN, precision=HIGH, preferred_element_type=F32)


def mask_of(ancestors, row_start, rows):
    numbers = row_start + jnp.arange(rows, dtype=jnp.int32)
    return jnp.any(ancestors[:, None] == numbers[None, :], axis=0).astype(F32)


def reduce_plan(known_inverse, first_factor, first_corner, first_ancestors, second_factor, second_link, second_corner, second_ancestors):
    groups, share_rows, block_rows = known_inverse.shape
    half_width = second_corner.shape[1]
    col_index = lax.axis_index("col")
    row_start = lax.axis_index("row") * block_rows
    first_mask = mask_of(first_ancestors, row_start, block_rows)[:, None]
    second_mask = mask_of(second_ancestors, row_start, block_rows)[:, None]
    first_masked = first_factor * first_mask
    second_masked = second_factor * second_mask
    share_start = col_index * share_rows
    first_piece = lax.dynamic_slice_in_dim(first_masked, share_start, share_rows, 0)
    second_piece = lax.dynamic_slice_in_dim(second_masked, share_start, share_rows, 0)
    columns = known_inverse.reshape(groups * share_rows, block_rows)
    first_partial = transposed_product(columns, lax.all_gather(first_piece, "row", axis=0, tiled=True))
    second_partial = transposed_product(columns, lax.all_gather(second_piece, "row", axis=0, tiled=True))
    first_image = lax.psum_scatter(first_partial, "col", scatter_dimension=1, tiled=True)
    first_column = -(first_image * first_mask)
    first_full = lax.all_gather(first_column, "col", axis=1, tiled=True)
    diagonal_partial = transposed_product(first_masked, first_column)
    corner_half = lax.dynamic_slice_in_dim(first_corner, col_index * half_width, half_width, 1)
    first_diagonal = corner_half - lax.psum(diagonal_partial, "row")
    diagonal_full = lax.all_gather(first_diagonal, "col", axis=1, tiled=True)
    second_image = lax.psum_scatter(second_partial, "col", scatter_dimension=1, tiled=True)
    link_half = lax.dynamic_slice_in_dim(second_link, col_index * half_width, half_width, 1)
    second_column = -((second_image + product(first_full, link_half)) * second_mask)
    second_half = lax.dynamic_slice_in_dim(second_masked, col_index * half_width, half_width, 1)
    cross_partial = transposed_product(first_full, second_half)
    closing_partial = transposed_product(second_masked, second_column)
    cross_total, closing_total = lax.psum((cross_partial, closing_partial), "row")
    second_cross = -(cross_total + product(diagonal_full, link_half))
    second_diagonal = second_corner - closing_total - transposed_product(second_link, second_cross)
    return (first_column, first_diagonal, second_column, second_cross, second_diagonal)


def dot(left, right, dims):
    return lax.dot_general(left, right, dims, preferred_element_type=F32)


def split(value):
    high = value.astype(BF16)
    return high, (value - high.astype(F32)).astype(BF16)


def dot3(left, right, dims):
    (lh, ll), (rh, rl) = left, right
    return dot(lh, rh, dims) + (dot(lh, rl, dims) + dot(ll, rh, dims))


def dot2(exact, right, dims, flip=False):
    rh, rl = right
    if flip:
        return dot(rh, exact, dims) + dot(rl, exact, dims)
    return dot(exact, rh, dims) + dot(exact, rl, dims)


def slot_codes(mask):
    block = mask.shape[1]
    before = (lax.broadcasted_iota(jnp.int32, (block, block), 0) < lax.broadcasted_iota(jnp.int32, (block, block), 1)).astype(BF16)
    rank = dot(mask.astype(BF16), before, NN)
    return jnp.where(mask > 0, rank, -1.0).astype(jnp.int32)


def picker(code_row, slots, offset=0):
    block = code_row.shape[1]
    at = lax.broadcasted_iota(jnp.int32, (slots, block), 0) - offset
    return ((at == code_row) & (code_row >= 0)).astype(BF16)


def prepare_kernel(cap, place, mask1, mask2, first, second, link, mine, theirs, out, out_half, code, m2, cols):
    row, col = place[0], place[1]
    groups, share, block = mine.shape
    width = first.shape[1]
    code[...] = slot_codes(mask1[...])
    m2[...] = mask2[...]
    pick = picker(code[pl.ds(row, 1), :], cap)
    pick2 = (pick.astype(F32) * m2[pl.ds(row, 1), :]).astype(BF16)
    first_c = dot2(pick, split(first[...]), NN)
    second_c = dot2(pick2, split(second[...]), NN)
    out[:, :width] = first_c
    out[:, width : 2 * width] = second_c - dot3(split(first_c), split(link[...]), NN)
    for g in range(groups):
        base = g * block
        cols[pl.ds(pl.multiple_of(base + col * share, share), share), :] = mine[g]
        cols[pl.ds(pl.multiple_of(base + (1 - col) * share, share), share), :] = theirs[g]
    half = dot2(pick, split(cols[...]), NT)
    wide = out.shape[1] - 2 * width
    total = jnp.zeros((cap, wide), F32)
    for g in range(groups):
        spread = picker(code[g : g + 1, :], wide, g * cap)
        total += dot2(spread, split(half[:, g * block : (g + 1) * block]), NT, flip=True)
    out[:, 2 * width :] = total
    half_cap = cap // 2
    out_half[...] = out[pl.ds(pl.multiple_of(col * half_cap, 8), half_cap), :]


def finish_kernel(cap, sources, *refs):
    place, mask1, mask2 = refs[:3]
    own = refs[3]
    n = len(sources)
    near, far = refs[4 : 4 + n], refs[4 + n : 4 + 2 * n]
    corner1, corner2, cross0, diag0 = refs[4 + 2 * n : 8 + 2 * n]
    outs = refs[8 + 2 * n : 13 + 2 * n]
    ft, known, code, m2, c1, g1, c2, xx, g2, sems = refs[13 + 2 * n :]
    row, col = place[0], place[1]
    width = own.shape[1] - known.shape[1]
    width //= 2
    half_width = width // 2
    half = cap // 2

    code[...] = slot_codes(mask1[...])
    m2[...] = mask2[...]

    def put(value, start, rows):
        at = pl.ds(pl.multiple_of(start, 8), rows)
        ft[at, :] = value[:, : 2 * width]
        known[at, :] = value[:, 2 * width :]

    put(own[...], row * cap, cap)
    for source, a, b in zip(sources, near, far):
        base = source(row) * cap
        put(a[...], base + col * half, half)
        put(b[...], base + (1 - col) * half, half)

    start = pl.multiple_of(col * half_width, half_width)
    right_f = split(ft[:, pl.ds(start, half_width)])
    right_t = split(ft[:, pl.ds(pl.multiple_of(width + start, half_width), half_width)])
    k = split(known[...])
    image_f = dot3(k, right_f, NN)
    image_t = dot3(k, right_t, NN)
    c1[...] = image_f
    c2[...] = image_t
    mine = pl.ds(pl.multiple_of(row * cap, 8), cap)
    own_f, own_t = split(c1[mine, :]), split(c2[mine, :])
    pick = picker(code[pl.ds(row, 1), :], cap)
    pick2 = (pick.astype(F32) * m2[pl.ds(row, 1), :]).astype(BF16)
    block = code.shape[1]
    c1[:block, :] = -dot2(pick, own_f, TN)
    c2[:block, :] = -dot2(pick2, own_t, TN)
    copies = [
        pltpu.make_async_copy(c1.at[:block], outs[0], sems.at[0]),
        pltpu.make_async_copy(c2.at[:block], outs[2], sems.at[2]),
    ]
    for copy in copies:
        copy.start()
    image_f, image_t = split(image_f), split(image_t)
    left_f = split(ft[:, :width])
    left_t = split(ft[:, width:])
    g1[...] = corner1[...] + dot3(left_f, image_f, TN)
    copies.append(pltpu.make_async_copy(g1, outs[1], sems.at[1]))
    copies[-1].start()
    xx[...] = dot3(left_f, image_t, TN) - cross0[...]
    copies.append(pltpu.make_async_copy(xx, outs[3], sems.at[3]))
    copies[-1].start()
    g2[...] = corner2[...] + (diag0[...] + dot3(left_t, image_t, TN))
    copies.append(pltpu.make_async_copy(g2, outs[4], sems.at[4]))
    copies[-1].start()
    for copy in copies:
        copy.wait()


def side_kernel(place, corner, link, corner_half, cross0, diag0, link_half):
    half_width = cross0.shape[1]
    start = pl.multiple_of(place[1] * half_width, half_width)
    corner_half[...] = corner[:, pl.ds(start, half_width)]
    link_half[...] = link[:, pl.ds(start, half_width)]
    value = dot3(split(corner[...]), split(link_half[...]), NN)
    cross0[...] = value
    diag0[...] = dot3(split(link[...]), split(value), TN)


def gather_branch(cap, n, place, mask1, mask2, known_inverse, theirs, first_factor, second_factor, second_link, first_corner, second_corner):
    _, _, block = known_inverse.shape
    width = first_factor.shape[1]
    half_width = second_corner.shape[1]
    wide = -(-n * cap // 128) * 128
    cost = pl.CostEstimate(flops=2 * cap * width * (width + n * block), bytes_accessed=4 * width * width * 2, transcendentals=0)
    payload, own_half = pl.pallas_call(
        functools.partial(prepare_kernel, cap),
        out_shape=(jax.ShapeDtypeStruct((cap, 2 * width + wide), F32), jax.ShapeDtypeStruct((cap // 2, 2 * width + wide), F32)),
        in_specs=[SMEM] + [VMEM] * 7,
        out_specs=(VMEM, VMEM),
        scratch_shapes=[
            pltpu.VMEM((n, block), jnp.int32),
            pltpu.VMEM((n, block), F32),
            pltpu.VMEM((n * block, block), F32),
        ],
        cost_estimate=cost,
        name="prepare",
    )(place, mask1, mask2, first_factor, second_factor, second_link, known_inverse, theirs)

    ring = [(r, (r + 2) % n) for r in range(n)]
    pair = [(r, r ^ 1) for r in range(n)]
    swap = [(0, 1), (1, 0)]

    along = [own_half]
    sources, near = [], []
    across = [lax.ppermute(own_half, "row", pair)]
    for _ in range(1, n // 2):
        along.append(lax.ppermute(along[-1], "row", ring))
        across.append(lax.ppermute(along[-1], "row", pair))
    far = []
    for step in range(n // 2):
        if step:
            near.append(along[step])
            far.append(lax.ppermute(along[step], "col", swap))
            sources.append(lambda r, s=step: lax.rem(r - 2 * s + n, n))
        near.append(across[step])
        far.append(lax.ppermute(across[step], "col", swap))
        sources.append(lambda r, s=step: lax.rem(lax.rem(r, 2) * -2 + 1 + r - 2 * s + n, n))

    square = jax.ShapeDtypeStruct((width, half_width), F32)
    corner_half, cross0, diag0 = pl.pallas_call(
        side_kernel,
        out_shape=(square, square, square),
        in_specs=[SMEM] + [VMEM] * 2,
        out_specs=(VMEM, VMEM, VMEM),
        scratch_shapes=[pltpu.VMEM((width, half_width), F32)],
        cost_estimate=pl.CostEstimate(flops=12 * width * width * half_width, bytes_accessed=20 * width * width, transcendentals=0),
        name="side",
    )(place, first_corner, second_link)

    rows = wide
    outs = (
        jax.ShapeDtypeStruct((block, half_width), F32),
        jax.ShapeDtypeStruct((width, half_width), F32),
        jax.ShapeDtypeStruct((block, half_width), F32),
        jax.ShapeDtypeStruct((width, half_width), F32),
        jax.ShapeDtypeStruct((width, half_width), F32),
    )
    m = len(near)
    cost = pl.CostEstimate(flops=2 * 3 * (rows * rows * width + 3 * width * rows * half_width), bytes_accessed=4 * rows * (2 * width + wide), transcendentals=0)
    return pl.pallas_call(
        functools.partial(finish_kernel, cap, sources),
        out_shape=outs,
        in_specs=[SMEM] + [VMEM] * (7 + 2 * m),
        out_specs=[ANY] * 5,
        scratch_shapes=[
            pltpu.VMEM((rows, 2 * width), F32),
            pltpu.VMEM((rows, wide), F32),
            pltpu.VMEM((n, block), jnp.int32),
            pltpu.VMEM((n, block), F32),
            pltpu.VMEM((max(rows, block), half_width), F32),
            pltpu.VMEM((width, half_width), F32),
            pltpu.VMEM((max(rows, block), half_width), F32),
            pltpu.VMEM((width, half_width), F32),
            pltpu.VMEM((width, half_width), F32),
            pltpu.SemaphoreType.DMA((5,)),
        ],
        compiler_params=pltpu.CompilerParams(vmem_limit_bytes=48 << 20),
        cost_estimate=cost,
        name="finish",
    )(place, mask1, mask2, payload, *near, *far, corner_half, second_corner, cross0, diag0)


def gather_plan(n, known_inverse, first_factor, first_corner, first_ancestors, second_factor, second_link, second_corner, second_ancestors):
    _, _, block = known_inverse.shape
    row, col = lax.axis_index("row"), lax.axis_index("col")
    place = jnp.stack([row, col]).astype(jnp.int32)
    theirs = lax.ppermute(known_inverse, "col", [(0, 1), (1, 0)])
    mask1 = mask_of(first_ancestors, 0, n * block).reshape(n, block)
    mask2 = mask_of(second_ancestors, 0, n * block).reshape(n, block)
    mean = -(-first_ancestors.shape[0] // n)
    cap = -(-mean * 5 // 64) * 16
    operands = (place, mask1, mask2, known_inverse, theirs, first_factor, second_factor, second_link, first_corner, second_corner)

    def branch(slots):
        def run(*values):
            return gather_branch(slots, n, *values)

        return run

    if cap >= block:
        return branch(block)(*operands)
    fits = jnp.max(jnp.sum(mask1, axis=1)) <= cap
    return lax.cond(fits, branch(cap), branch(block), *operands)


def solution(mesh):
    n = mesh.shape["row"]

    def on_device(known_inverse, *rest):
        _, _, block = known_inverse.shape
        width = rest[0].shape[1]
        if n % 2 == 0 and mesh.shape["col"] == 2 and (n * block) ** 2 <= 12 * width**2:
            return gather_plan(n, known_inverse, *rest)
        return reduce_plan(known_inverse, *rest)

    return jax.shard_map(
        on_device,
        mesh=mesh,
        in_specs=(
            P("pole", "col", "row"),
            P(("pole", "row"), None),
            P("pole", None),
            P("pole"),
            P(("pole", "row"), None),
            P("pole", None),
            P("pole", "col"),
            P("pole"),
        ),
        out_specs=(
            P(("pole", "row"), "col"),
            P("pole", "col"),
            P(("pole", "row"), "col"),
            P("pole", "col"),
            P("pole", "col"),
        ),
        check_vma=False,
    )
```

```python
import functools

import jax
import jax.numpy as jnp
from jax import lax
from jax.experimental import pallas as pl
from jax.experimental.pallas import tpu as pltpu
from jax.sharding import PartitionSpec as P


HIGH = lax.Precision.HIGHEST
F32, BF16 = jnp.float32, jnp.bfloat16
LANES = 128
NN = (((1,), (0,)), ((), ()))
NT = (((1,), (1,)), ((), ()))
TN = (((0,), (0,)), ((), ()))
VMEM = pl.BlockSpec(memory_space=pltpu.VMEM)
SMEM = pl.BlockSpec(memory_space=pltpu.SMEM)
ANY = pl.BlockSpec(memory_space=pl.ANY)


def product(left, right):
    return jnp.dot(left, right, precision=HIGH, preferred_element_type=F32)


def transposed_product(left, right):
    return lax.dot_general(left, right, TN, precision=HIGH, preferred_element_type=F32)


def mask_of(ancestors, row_start, rows):
    numbers = row_start + jnp.arange(rows, dtype=jnp.int32)
    return jnp.any(ancestors[:, None] == numbers[None, :], axis=0).astype(F32)


def reduce_plan(known_inverse, first_factor, first_corner, first_ancestors, second_factor, second_link, second_corner, second_ancestors):
    groups, share_rows, block_rows = known_inverse.shape
    half_width = second_corner.shape[1]
    col_index = lax.axis_index("col")
    row_start = lax.axis_index("row") * block_rows
    first_mask = mask_of(first_ancestors, row_start, block_rows)[:, None]
    second_mask = mask_of(second_ancestors, row_start, block_rows)[:, None]
    first_masked = first_factor * first_mask
    second_masked = second_factor * second_mask
    share_start = col_index * share_rows
    first_piece = lax.dynamic_slice_in_dim(first_masked, share_start, share_rows, 0)
    second_piece = lax.dynamic_slice_in_dim(second_masked, share_start, share_rows, 0)
    columns = known_inverse.reshape(groups * share_rows, block_rows)
    first_partial = transposed_product(columns, lax.all_gather(first_piece, "row", axis=0, tiled=True))
    second_partial = transposed_product(columns, lax.all_gather(second_piece, "row", axis=0, tiled=True))
    first_image = lax.psum_scatter(first_partial, "col", scatter_dimension=1, tiled=True)
    first_column = -(first_image * first_mask)
    first_full = lax.all_gather(first_column, "col", axis=1, tiled=True)
    diagonal_partial = transposed_product(first_masked, first_column)
    corner_half = lax.dynamic_slice_in_dim(first_corner, col_index * half_width, half_width, 1)
    first_diagonal = corner_half - lax.psum(diagonal_partial, "row")
    diagonal_full = lax.all_gather(first_diagonal, "col", axis=1, tiled=True)
    second_image = lax.psum_scatter(second_partial, "col", scatter_dimension=1, tiled=True)
    link_half = lax.dynamic_slice_in_dim(second_link, col_index * half_width, half_width, 1)
    second_column = -((second_image + product(first_full, link_half)) * second_mask)
    second_half = lax.dynamic_slice_in_dim(second_masked, col_index * half_width, half_width, 1)
    cross_partial = transposed_product(first_full, second_half)
    closing_partial = transposed_product(second_masked, second_column)
    cross_total, closing_total = lax.psum((cross_partial, closing_partial), "row")
    second_cross = -(cross_total + product(diagonal_full, link_half))
    second_diagonal = second_corner - closing_total - transposed_product(second_link, second_cross)
    return (first_column, first_diagonal, second_column, second_cross, second_diagonal)


def dot(left, right, dims):
    return lax.dot_general(left, right, dims, preferred_element_type=F32)


def split(value):
    high = value.astype(BF16)
    return high, (value - high.astype(F32)).astype(BF16)


def dot3(left, right, dims):
    (lh, ll), (rh, rl) = left, right
    return dot(lh, rh, dims) + (dot(lh, rl, dims) + dot(ll, rh, dims))


def dot2(exact, right, dims, flip=False):
    rh, rl = right
    if flip:
        return dot(rh, exact, dims) + dot(rl, exact, dims)
    return dot(exact, rh, dims) + dot(exact, rl, dims)


def slot_codes(mask):
    block = mask.shape[1]
    before = (lax.broadcasted_iota(jnp.int32, (block, block), 0) < lax.broadcasted_iota(jnp.int32, (block, block), 1)).astype(BF16)
    rank = dot(mask.astype(BF16), before, NN)
    return jnp.where(mask > 0, rank, -1.0).astype(jnp.int32)


def marks(ancestors, n, block):
    count = ancestors.shape[1]
    group = lax.div(ancestors, block)
    inside = ancestors - group * block
    groups = (lax.broadcasted_iota(jnp.int32, (n, count), 0) == group).astype(BF16)
    insides = (lax.broadcasted_iota(jnp.int32, (block, count), 0) == inside).astype(BF16)
    return dot(groups, insides, NT)


def picker(code_row, slots, offset=0):
    block = code_row.shape[1]
    at = lax.broadcasted_iota(jnp.int32, (slots, block), 0) - offset
    return ((at == code_row) & (code_row >= 0)).astype(BF16)


def rows_at(start, size, step=8):
    return pl.ds(pl.multiple_of(start, step), size)


def factors_kernel(cap, n, anc1, anc2, first, second, link, out, code, m2, most):
    row = lax.axis_index("row")
    block, width = first.shape
    mask1 = marks(anc1[...], n, block)
    code[...] = slot_codes(mask1)
    m2[...] = marks(anc2[...], n, block)
    most[0, 0] = jnp.max(jnp.sum(mask1, axis=1, keepdims=True)).astype(jnp.int32)
    pick = picker(code[pl.ds(row, 1), :], cap)
    pick2 = (pick.astype(F32) * m2[pl.ds(row, 1), :]).astype(BF16)
    first_c = dot2(pick, split(first[...]), NN)
    out[:, :width] = first_c
    out[:, width:] = dot2(pick2, split(second[...]), NN) - dot3(split(first_c), split(link[...]), NN)


def place_of(row, n):
    return jnp.where(lax.rem(row, 2) == 0, lax.div(row, 2), n - 1 - lax.div(row, 2))


def row_of(place, n):
    return jnp.where(place < n // 2, 2 * place, 2 * (n - 1 - place) + 1)


def chunks_of(lanes):
    return -(-lanes // LANES)


def arrivals_of(n):
    return [0] + [sign * k for k in range(1, n // 2) for sign in (-1, 1)] + [n // 2]


def payload_kernel(cap, n, counts, code, factors, mine, theirs, own, up, down, cols, images, own_ud):
    row, col = lax.axis_index("row"), lax.axis_index("col")
    groups, share, block = mine.shape
    both, half = factors.shape[1], cap // 2
    for g in range(groups):
        base = g * block
        cols[rows_at(base + col * share, share), :] = mine[g]
        cols[rows_at(base + (1 - col) * share, share), :] = theirs[g]
    pick = picker(code[pl.ds(row, 1), :], cap)
    images[...] = dot2(pick, split(cols[...]), NT)
    arrivals = arrivals_of(n)
    place = place_of(row, n)
    own_ud[...] = jnp.zeros(own_ud.shape, F32)
    for d in range(n):
        g = row_of(lax.rem(place + d, n), n)
        spread = picker(code[pl.ds(g, 1), :], cap)
        image = images[:, pl.ds(pl.multiple_of(g * block, block), block)]
        value = dot2(spread, split(image), NT, flip=True)
        x = arrivals.index(d if d <= n // 2 else d - n)
        own[:, x * cap : (x + 1) * cap] = value
        for way, slot in ((0, (n - d) % n), (1, d)):
            if slot < counts[way]:
                own_ud[way, :, slot * cap : (slot + 1) * cap] = value
    mine_rows = rows_at(col * half, half)
    for way, out in ((0, up), (1, down)):
        for c in range(both // LANES):
            out[c * half : (c + 1) * half, :] = factors[mine_rows, c * LANES : (c + 1) * LANES]
        for c in range(chunks_of(counts[way] * cap)):
            at = both // LANES + c
            out[at * half : (at + 1) * half, :] = own_ud[way, mine_rows, c * LANES : (c + 1) * LANES]


def side_kernel(corner, link, cross0, diag0, link_half):
    half_width = cross0.shape[1]
    start = pl.multiple_of(lax.axis_index("col") * half_width, half_width)
    link_half[...] = link[:, pl.ds(start, half_width)]
    value = dot3(split(corner[...]), split(link_half[...]), NN)
    cross0[...] = value
    diag0[...] = dot3(split(link[...]), split(value), TN)


def assemble(cap, flat, blk, k):
    col = lax.axis_index("col")
    half = cap // 2
    for value, side in zip(flat, (col, 1 - col)):
        for c in range(value.shape[0] // half):
            blk[rows_at(k * cap + side * half, half), c * LANES : (c + 1) * LANES] = value[c * half : (c + 1) * half, :]


def columns(both, half_width):
    start = lax.axis_index("col") * half_width
    f_at = pl.ds(pl.multiple_of(start, half_width), half_width)
    t_at = pl.ds(pl.multiple_of(both // 2 + start, half_width), half_width)
    return f_at, t_at


def pairs(size, values, lh, ll, rh, rl):
    both, half_width = lh.shape[1], rh.shape[1] // 2
    width = both // 2
    lh[size:, :], ll[size:, :] = split(values)
    f_at, t_at = columns(both, half_width)
    for left, right in ((lh, rh), (ll, rl)):
        for lanes, at in ((slice(0, half_width), f_at), (slice(half_width, 2 * half_width), t_at)):
            right[:size, lanes] = left[size:, at]
            right[size:, lanes] = left[:size, at]
    cross = dot3((lh[:, :width], ll[:, :width]), (rh[...], rl[...]), TN)
    close = dot3((lh[:, width:], ll[:, width:]), (rh[:, half_width:], rl[:, half_width:]), TN)
    return cross, close


def ahead(pieces, slots):
    lanes = slice(slots[0] * LANES, (slots[-1] + 1) * LANES)
    total = None
    for fth, ftl, kh, kl in pieces:
        value = dot3((kh[:, lanes], kl[:, lanes]), (fth[...], ftl[...]), TN)
        total = value if total is None else total + value
    return total


def update_kernel(cap, n, k, *refs):
    arrivals = arrivals_of(n)
    fresh, final = k == 1, k == n // 2 - 1
    if fresh:
        (factors, own), refs = refs[:2], refs[2:]
        old = ()
    else:
        old_v, old_ab, old_ee = refs[:3]
        refs = refs[3:]
        old = [refs[4 * m : 4 * m + 4] for m in range(k - 1)]
        refs = refs[4 * (k - 1) :]
        if final:
            own, refs = refs[0], refs[1:]
    up, down, refs = refs[:2], refs[2:4], refs[4:]
    fth, ftl, kh, kl, ab, ee, v_next, *refs = refs
    if final:
        image, *refs = refs
    blk, middle, lh, ll, rh, rl = refs
    both = fth.shape[1]
    news = ([0] if fresh else []) + [2 * k - 1, 2 * k]
    size = cap * len(news)
    if fresh:
        blk[:cap, :both] = factors[...]
    base = len(news) - 2
    assemble(cap, up, blk, base)
    assemble(cap, down, blk, base + 1)
    middle[...] = jnp.zeros(middle.shape, F32)
    kh[...] = jnp.zeros(kh.shape, BF16)
    kl[...] = jnp.zeros(kl.shape, BF16)
    for a, x in enumerate(news):
        rows = slice(a * cap, (a + 1) * cap)
        for y in range(x, n):
            if x == 0:
                value = own[:, y * cap : (y + 1) * cap]
            else:
                way = -1 if arrivals[x] < 0 else 1
                slot = (way * (arrivals[y] - arrivals[x])) % n
                if slot >= n - 2 * k + (1 if way < 0 or slot == 0 else 0):
                    continue
                value = blk[rows, both + slot * cap : both + (slot + 1) * cap]
            if y in news:
                b = news.index(y)
                middle[rows, b * cap : (b + 1) * cap] = value * 0.5 if y == x else value
            else:
                kh[rows, y * LANES : y * LANES + cap], kl[rows, y * LANES : y * LANES + cap] = split(value)
    sh, sl = split(blk[:, :both])
    fth[...], ftl[...] = sh, sl
    lh[:size, :], ll[:size, :] = sh, sl
    values = dot3(split(middle[...]), (sh, sl), NN)
    if not fresh:
        values = values + jnp.concatenate([old_v[:cap, :], old_v[LANES : LANES + cap, :]], axis=0)
    cross, close = pairs(size, values, lh, ll, rh, rl)
    if fresh:
        ab[...], ee[...] = cross, close
    else:
        ab[...] = old_ab[...] + cross
        ee[...] = old_ee[...] + close
    pieces = [*old, (fth, ftl, kh, kl)]
    v_next[...] = ahead(pieces, [2 * k + 1] if final else [2 * k + 1, 2 * k + 2])
    if final:
        f_at, t_at = columns(both, ee.shape[1])
        start = 0
        total_f = total_t = None
        for ph, pl_, _, _ in pieces:
            stop = start + ph.shape[0]
            part = split(own[:, start:stop])
            value_f = dot3(part, (ph[:, f_at], pl_[:, f_at]), NN)
            value_t = dot3(part, (ph[:, t_at], pl_[:, t_at]), NN)
            total_f = value_f if total_f is None else total_f + value_f
            total_t = value_t if total_t is None else total_t + value_t
            start = stop
        image[:, : ee.shape[1]] = total_f
        image[:, ee.shape[1] :] = total_t


def last_kernel(cap, n, up, down, up_far, down_far, old_v, old_ab, old_ee, image, own, code, m2, corner1, corner2, cross0, diag0, *refs):
    c1, g1, c2, xx, g2, flat, flat_far, blk, lh, ll, rh, rl, c1_v, g1_v, c2_v, xx_v, g2_v, corner1_v, corner2_v, cross0_v, diag0_v, sems = refs
    row, col = lax.axis_index("row"), lax.axis_index("col")
    both, half_width = lh.shape[1], old_ee.shape[1]
    half_at = pl.ds(pl.multiple_of(col * half_width, half_width), half_width)
    loads = [
        pltpu.make_async_copy(corner1.at[:, half_at], corner1_v, sems.at[5]),
        pltpu.make_async_copy(corner2, corner2_v, sems.at[6]),
        pltpu.make_async_copy(cross0, cross0_v, sems.at[7]),
        pltpu.make_async_copy(diag0, diag0_v, sems.at[8]),
    ]
    for load in loads:
        load.start()
    cut = up.shape[0]
    flat[:cut, :], flat[cut:, :] = up[...], down[...]
    flat_far[:cut, :], flat_far[cut:, :] = up_far[...], down_far[...]
    assemble(cap, (flat, flat_far), blk, 0)
    sh, sl = split(blk[:, :both])
    lh[:cap, :], ll[:cap, :] = sh, sl
    values = dot3(split(blk[:, both : both + cap] * 0.5), (sh, sl), NN) + old_v[:cap, :]
    cross, close = pairs(cap, values, lh, ll, rh, rl)
    for load in loads:
        load.wait()
    copies = []

    def send(value, ref, out):
        ref[...] = value
        copies.append(pltpu.make_async_copy(ref, out, sems.at[len(copies)]))
        copies[-1].start()

    send(corner1_v[...] + (old_ab[:, :half_width] + cross[:, :half_width]), g1_v, g1)
    send(old_ab[:, half_width:] + cross[:, half_width:] - cross0_v[...], xx_v, xx)
    send(corner2_v[...] + (diag0_v[...] + (old_ee[...] + close)), g2_v, g2)
    k = split(own[:, (n - 1) * cap :])
    pick = picker(code[pl.ds(row, 1), :], cap)
    pick2 = (pick.astype(F32) * m2[pl.ds(row, 1), :]).astype(BF16)
    f_at, t_at = columns(both, half_width)
    image_f = image[:, :half_width] + dot3(k, (lh[:cap, f_at], ll[:cap, f_at]), NN)
    send(-dot2(pick, split(image_f), TN), c1_v, c1)
    image_t = image[:, half_width:] + dot3(k, (lh[:cap, t_at], ll[:cap, t_at]), NN)
    send(-dot2(pick2, split(image_t), TN), c2_v, c2)
    for copy in copies:
        copy.wait()


def call_factors(cap, n, anc1, anc2, first_factor, second_factor, second_link):
    block, width = first_factor.shape
    return pl.pallas_call(
        functools.partial(factors_kernel, cap, n),
        out_shape=(
            jax.ShapeDtypeStruct((cap, 2 * width), F32),
            jax.ShapeDtypeStruct((n, block), jnp.int32),
            jax.ShapeDtypeStruct((n, block), F32),
            jax.ShapeDtypeStruct((1, 1), jnp.int32),
        ),
        in_specs=[VMEM] * 5,
        out_specs=(VMEM, VMEM, VMEM, SMEM),
        cost_estimate=pl.CostEstimate(flops=6 * cap * width * width, bytes_accessed=4 * width * (2 * block + width), transcendentals=0),
        name="factors",
    )(anc1, anc2, first_factor, second_factor, second_link)


def call_payload(cap, n, code, factors, mine, theirs):
    _, _, block = mine.shape
    both, half = factors.shape[1], cap // 2
    counts = (n - 1, n - 2)
    flats = [jax.ShapeDtypeStruct(((both // LANES + chunks_of(count * cap)) * half, LANES), F32) for count in counts]
    return pl.pallas_call(
        functools.partial(payload_kernel, cap, n, counts),
        out_shape=(jax.ShapeDtypeStruct((cap, n * cap), F32), *flats),
        in_specs=[VMEM] * 4,
        out_specs=(VMEM,) * 3,
        scratch_shapes=[
            pltpu.VMEM((n * block, block), F32),
            pltpu.VMEM((cap, n * block), F32),
            pltpu.VMEM((2, cap, chunks_of(counts[0] * cap) * LANES), F32),
        ],
        cost_estimate=pl.CostEstimate(flops=8 * cap * block * n * block, bytes_accessed=8 * n * block * block, transcendentals=0),
        name="payload",
    )(code, factors, mine, theirs)


def gather_branch(cap, n, factors, code, m2, own, own_up, own_down, second_link, first_corner, second_corner):
    block = code.shape[1]
    width = second_link.shape[0]
    half_width = second_corner.shape[1]
    half, both = cap // 2, 2 * width
    square = jax.ShapeDtypeStruct((width, half_width), F32)
    tall = jax.ShapeDtypeStruct((block, half_width), F32)

    order = [*range(0, n, 2), *range(n - 1, 0, -2)]
    ups = [(order[k], order[(k + 1) % n]) for k in range(n)]
    downs = [(b, a) for a, b in ups]
    swap = [(0, 1), (1, 0)]

    def scratch_of(blocks):
        size = cap * blocks
        return [
            pltpu.VMEM((2 * size, both), BF16),
            pltpu.VMEM((2 * size, both), BF16),
            pltpu.VMEM((2 * size, 2 * half_width), BF16),
            pltpu.VMEM((2 * size, 2 * half_width), BF16),
        ]

    params = pltpu.CompilerParams(vmem_limit_bytes=40 << 20)
    cross0, diag0 = pl.pallas_call(
        side_kernel,
        out_shape=(square, square),
        in_specs=[VMEM] * 2,
        out_specs=(VMEM, VMEM),
        scratch_shapes=[pltpu.VMEM((width, half_width), F32)],
        cost_estimate=pl.CostEstimate(flops=12 * width * width * half_width, bytes_accessed=20 * width * width, transcendentals=0),
        name="side",
    )(first_corner, second_link)

    def flat_rows(count):
        return (both // LANES + chunks_of(count * cap)) * half

    up, down = own_up, own_down
    pieces, state, image = [], (), ()
    for k in range(1, n // 2):
        up = lax.ppermute(up[: flat_rows(n + 1 - 2 * k)], "row", ups)
        down = lax.ppermute(down[: flat_rows(n - 2 * k)], "row", downs)
        up_far, down_far = lax.ppermute(up, "col", swap), lax.ppermute(down, "col", swap)
        fresh, final = k == 1, k == n // 2 - 1
        blocks = 3 if fresh else 2
        size = blocks * cap
        ins = [factors, own] if fresh else [*state, *(array for piece in pieces for array in piece)]
        if final and not fresh:
            ins.append(own)
        ins += [up, up_far, down, down_far]
        half_piece = jax.ShapeDtypeStruct((size, both), BF16)
        outs = [half_piece, half_piece] + [jax.ShapeDtypeStruct((size, n * LANES), BF16)] * 2
        outs += [jax.ShapeDtypeStruct((width, 2 * half_width), F32), square]
        outs += [jax.ShapeDtypeStruct(((1 if final else 2) * LANES, both), F32)]
        if final:
            outs += [jax.ShapeDtypeStruct((cap, 2 * half_width), F32)]
        results = pl.pallas_call(
            functools.partial(update_kernel, cap, n, k),
            out_shape=tuple(outs),
            in_specs=[VMEM] * len(ins),
            out_specs=(VMEM,) * len(outs),
            scratch_shapes=[pltpu.VMEM((size, both + chunks_of((n - 1) * cap) * LANES), F32), pltpu.VMEM((size, size), F32)] + scratch_of(blocks),
            compiler_params=params,
            cost_estimate=pl.CostEstimate(flops=6 * size * width * (4 * size + 6 * half_width), bytes_accessed=4 * size * width * 8, transcendentals=0),
        )(*ins)
        pieces.append(results[:4])
        ab, ee, v_next = results[4:7]
        state = (v_next, ab, ee)
        image = results[7:]
    rows = flat_rows(1)
    cut = -(-rows // 16) * 8
    k = n // 2
    up = lax.ppermute(up[:cut], "row", ups)
    down = lax.ppermute(down[cut:rows], "row", downs)
    up_far, down_far = lax.ppermute(up, "col", swap), lax.ppermute(down, "col", swap)
    return pl.pallas_call(
        functools.partial(last_kernel, cap, n),
        out_shape=(tall, square, tall, square, square),
        in_specs=[VMEM] * 11 + [ANY] * 4,
        out_specs=(ANY,) * 5,
        scratch_shapes=[pltpu.VMEM((rows, LANES), F32)] * 2
        + [pltpu.VMEM((cap, both + chunks_of(cap) * LANES), F32)]
        + scratch_of(1)
        + [pltpu.VMEM(shape.shape, F32) for shape in (tall, square, tall, square, square)]
        + [pltpu.VMEM(square.shape, F32)] * 4
        + [pltpu.SemaphoreType.DMA((9,))],
        compiler_params=params,
        cost_estimate=pl.CostEstimate(flops=6 * cap * width * (2 * width + 6 * half_width), bytes_accessed=4 * width * width * 5, transcendentals=0),
        name="last",
    )(up, down, up_far, down_far, *state, *image, own, code, m2, first_corner, second_corner, cross0, diag0)


def gather_plan(n, known_inverse, first_factor, first_corner, first_ancestors, second_factor, second_link, second_corner, second_ancestors):
    _, _, block = known_inverse.shape
    theirs = lax.ppermute(known_inverse, "col", [(0, 1), (1, 0)])
    anc1, anc2 = first_ancestors[None, :], second_ancestors[None, :]
    mean = -(-first_ancestors.shape[0] // n)
    cap = min(-(-mean * 5 // 64) * 16, block)
    factors, code, m2, most = call_factors(cap, n, anc1, anc2, first_factor, second_factor, second_link)
    own = call_payload(cap, n, code, factors, known_inverse, theirs)

    def compact(own, factors, code, m2, known_inverse, theirs, anc1, anc2, first_factor, second_factor, second_link, first_corner, second_corner):
        return gather_branch(cap, n, factors, code, m2, *own, second_link, first_corner, second_corner)

    def general(own, factors, code, m2, known_inverse, theirs, anc1, anc2, first_factor, second_factor, second_link, first_corner, second_corner):
        factors, code, m2, _ = call_factors(block, n, anc1, anc2, first_factor, second_factor, second_link)
        own = call_payload(block, n, code, factors, known_inverse, theirs)
        return gather_branch(block, n, factors, code, m2, *own, second_link, first_corner, second_corner)

    operands = (own, factors, code, m2, known_inverse, theirs, anc1, anc2, first_factor, second_factor, second_link, first_corner, second_corner)
    if cap == block:
        return compact(*operands)
    return lax.cond(most[0, 0] <= cap, compact, general, *operands)


def solution(mesh):
    n = mesh.shape["row"]

    def on_device(known_inverse, *rest):
        _, _, block = known_inverse.shape
        width = rest[0].shape[1]
        if n % 2 == 0 and n > 4 and block % LANES == 0 and mesh.shape["col"] == 2 and (n * block) ** 2 <= 12 * width**2:
            return gather_plan(n, known_inverse, *rest)
        return reduce_plan(known_inverse, *rest)

    return jax.shard_map(
        on_device,
        mesh=mesh,
        in_specs=(
            P("pole", "col", "row"),
            P(("pole", "row"), None),
            P("pole", None),
            P("pole"),
            P(("pole", "row"), None),
            P("pole", None),
            P("pole", "col"),
            P("pole"),
        ),
        out_specs=(
            P(("pole", "row"), "col"),
            P("pole", "col"),
            P(("pole", "row"), "col"),
            P("pole", "col"),
            P("pole", "col"),
        ),
        check_vma=False,
    )
```

```python
import functools

import jax
import jax.numpy as jnp
from jax import lax
from jax.experimental import pallas as pl
from jax.experimental.pallas import tpu as pltpu
from jax.sharding import PartitionSpec as P


HIGH = lax.Precision.HIGHEST
F32, BF16 = jnp.float32, jnp.bfloat16
LANES = 128
NN = (((1,), (0,)), ((), ()))
NT = (((1,), (1,)), ((), ()))
TN = (((0,), (0,)), ((), ()))
VMEM = pl.BlockSpec(memory_space=pltpu.VMEM)
SMEM = pl.BlockSpec(memory_space=pltpu.SMEM)
ANY = pl.BlockSpec(memory_space=pl.ANY)


def product(left, right):
    return jnp.dot(left, right, precision=HIGH, preferred_element_type=F32)


def transposed_product(left, right):
    return lax.dot_general(left, right, TN, precision=HIGH, preferred_element_type=F32)


def mask_of(ancestors, row_start, rows):
    numbers = row_start + jnp.arange(rows, dtype=jnp.int32)
    return jnp.any(ancestors[:, None] == numbers[None, :], axis=0).astype(F32)


def reduce_plan(known_inverse, first_factor, first_corner, first_ancestors, second_factor, second_link, second_corner, second_ancestors):
    groups, share_rows, block_rows = known_inverse.shape
    half_width = second_corner.shape[1]
    col_index = lax.axis_index("col")
    row_start = lax.axis_index("row") * block_rows
    first_mask = mask_of(first_ancestors, row_start, block_rows)[:, None]
    second_mask = mask_of(second_ancestors, row_start, block_rows)[:, None]
    first_masked = first_factor * first_mask
    second_masked = second_factor * second_mask
    share_start = col_index * share_rows
    first_piece = lax.dynamic_slice_in_dim(first_masked, share_start, share_rows, 0)
    second_piece = lax.dynamic_slice_in_dim(second_masked, share_start, share_rows, 0)
    columns = known_inverse.reshape(groups * share_rows, block_rows)
    first_partial = transposed_product(columns, lax.all_gather(first_piece, "row", axis=0, tiled=True))
    second_partial = transposed_product(columns, lax.all_gather(second_piece, "row", axis=0, tiled=True))
    first_image = lax.psum_scatter(first_partial, "col", scatter_dimension=1, tiled=True)
    first_column = -(first_image * first_mask)
    first_full = lax.all_gather(first_column, "col", axis=1, tiled=True)
    diagonal_partial = transposed_product(first_masked, first_column)
    corner_half = lax.dynamic_slice_in_dim(first_corner, col_index * half_width, half_width, 1)
    first_diagonal = corner_half - lax.psum(diagonal_partial, "row")
    diagonal_full = lax.all_gather(first_diagonal, "col", axis=1, tiled=True)
    second_image = lax.psum_scatter(second_partial, "col", scatter_dimension=1, tiled=True)
    link_half = lax.dynamic_slice_in_dim(second_link, col_index * half_width, half_width, 1)
    second_column = -((second_image + product(first_full, link_half)) * second_mask)
    second_half = lax.dynamic_slice_in_dim(second_masked, col_index * half_width, half_width, 1)
    cross_partial = transposed_product(first_full, second_half)
    closing_partial = transposed_product(second_masked, second_column)
    cross_total, closing_total = lax.psum((cross_partial, closing_partial), "row")
    second_cross = -(cross_total + product(diagonal_full, link_half))
    second_diagonal = second_corner - closing_total - transposed_product(second_link, second_cross)
    return (first_column, first_diagonal, second_column, second_cross, second_diagonal)


def dot(left, right, dims):
    return lax.dot_general(left, right, dims, preferred_element_type=F32)


def split(value):
    high = value.astype(BF16)
    return high, (value - high.astype(F32)).astype(BF16)


def dot3(left, right, dims):
    (lh, ll), (rh, rl) = left, right
    return dot(lh, rh, dims) + (dot(lh, rl, dims) + dot(ll, rh, dims))


def dot2(exact, right, dims, flip=False):
    rh, rl = right
    if flip:
        return dot(rh, exact, dims) + dot(rl, exact, dims)
    return dot(exact, rh, dims) + dot(exact, rl, dims)


def slot_codes(mask):
    block = mask.shape[1]
    before = (lax.broadcasted_iota(jnp.int32, (block, block), 0) < lax.broadcasted_iota(jnp.int32, (block, block), 1)).astype(BF16)
    rank = dot(mask.astype(BF16), before, NN)
    return jnp.where(mask > 0, rank, -1.0).astype(jnp.int32)


def marks(ancestors, n, block):
    count = ancestors.shape[1]
    group = lax.div(ancestors, block)
    inside = ancestors - group * block
    groups = (lax.broadcasted_iota(jnp.int32, (n, count), 0) == group).astype(BF16)
    insides = (lax.broadcasted_iota(jnp.int32, (block, count), 0) == inside).astype(BF16)
    return dot(groups, insides, NT)


def picker(code_row, slots, offset=0):
    block = code_row.shape[1]
    at = lax.broadcasted_iota(jnp.int32, (slots, block), 0) - offset
    return ((at == code_row) & (code_row >= 0)).astype(BF16)


def rows_at(start, size, step=8):
    return pl.ds(pl.multiple_of(start, step), size)


def fetch(pairs, sems):
    copies = [pltpu.make_async_copy(source, target, sems.at[k]) for k, (source, target) in enumerate(pairs)]
    for copy in copies:
        copy.start()
    return copies


def factors_kernel(cap, n, anc1_h, anc2_h, first_h, second_h, link_h, out, code, m2, most, anc1, anc2, first, second, link, sems):
    loads = fetch(((anc1_h, anc1), (anc2_h, anc2), (first_h, first), (second_h, second), (link_h, link)), sems)
    row = lax.axis_index("row")
    block, width = first.shape
    loads[0].wait()
    mask1 = marks(anc1[...], n, block)
    code[...] = slot_codes(mask1)
    most[...] = jnp.broadcast_to(jnp.max(jnp.sum(mask1, axis=1, keepdims=True), axis=0, keepdims=True), most.shape)
    loads[1].wait()
    m2[...] = marks(anc2[...], n, block)
    pick = picker(code[pl.ds(row, 1), :], cap)
    pick2 = (pick.astype(F32) * m2[pl.ds(row, 1), :]).astype(BF16)
    loads[2].wait()
    first_c = dot2(pick, split(first[...]), NN)
    out[:, :width] = first_c
    loads[3].wait()
    second_c = dot2(pick2, split(second[...]), NN)
    loads[4].wait()
    out[:, width:] = second_c - dot3(split(first_c), split(link[...]), NN)


def place_of(row, n):
    return jnp.where(lax.rem(row, 2) == 0, lax.div(row, 2), n - 1 - lax.div(row, 2))


def row_of(place, n):
    return jnp.where(place < n // 2, 2 * place, 2 * (n - 1 - place) + 1)


def chunks_of(lanes):
    return -(-lanes // LANES)


def arrivals_of(n):
    return [0] + [sign * k for k in range(1, n // 2) for sign in (-1, 1)] + [n // 2]


def payload_kernel(cap, n, counts, code, factors, mine_h, theirs, own, up, down, cols, images, own_ud, spreads, mine, sems):
    loads = fetch(((mine_h, mine),), sems)
    row, col = lax.axis_index("row"), lax.axis_index("col")
    groups, share, block = mine.shape
    both, half = factors.shape[1], cap // 2
    for g in range(groups):
        cols[rows_at(g * block + (1 - col) * share, share), :] = theirs[g]
        spreads[g * cap : (g + 1) * cap, :] = picker(code[g : g + 1, :], cap)
    own_ud[...] = jnp.zeros(own_ud.shape, F32)
    pick = picker(code[pl.ds(row, 1), :], cap)
    loads[0].wait()
    for g in range(groups):
        cols[rows_at(g * block + col * share, share), :] = mine[g]
    images[...] = dot2(pick, split(cols[...]), NT)
    arrivals = arrivals_of(n)
    place = place_of(row, n)
    for d in range(n):
        g = row_of(lax.rem(place + d, n), n)
        spread = spreads[rows_at(g * cap, cap, 16), :]
        image = images[:, pl.ds(pl.multiple_of(g * block, block), block)]
        value = dot2(spread, split(image), NT, flip=True)
        x = arrivals.index(d if d <= n // 2 else d - n)
        own[:, both + x * cap : both + (x + 1) * cap] = value
        for way, slot in ((0, (n - d) % n), (1, d)):
            if slot < counts[way]:
                own_ud[way, :, slot * cap : (slot + 1) * cap] = value
    own[:, :both] = factors[...]
    mine_rows = rows_at(col * half, half)
    for way, out in ((0, up), (1, down)):
        for c in range(both // LANES):
            out[c * half : (c + 1) * half, :] = factors[mine_rows, c * LANES : (c + 1) * LANES]
        for c in range(chunks_of(counts[way] * cap)):
            at = both // LANES + c
            out[at * half : (at + 1) * half, :] = own_ud[way, mine_rows, c * LANES : (c + 1) * LANES]


def side_kernel(corner, link, cross0, diag0, link_half):
    half_width = cross0.shape[1]
    start = pl.multiple_of(lax.axis_index("col") * half_width, half_width)
    link_half[...] = link[:, pl.ds(start, half_width)]
    value = dot3(split(corner[...]), split(link_half[...]), NN)
    cross0[...] = value
    diag0[...] = dot3(split(link[...]), split(value), TN)


def assemble(cap, flat, blk, k):
    col = lax.axis_index("col")
    half = cap // 2
    for value, side in zip(flat, (col, 1 - col)):
        for c in range(value.shape[0] // half):
            blk[rows_at(k * cap + side * half, half), c * LANES : (c + 1) * LANES] = value[c * half : (c + 1) * half, :]


def columns(both, half_width):
    start = lax.axis_index("col") * half_width
    f_at = pl.ds(pl.multiple_of(start, half_width), half_width)
    t_at = pl.ds(pl.multiple_of(both // 2 + start, half_width), half_width)
    return f_at, t_at


def pairs(size, values, lh, ll, rh, rl):
    both, half_width = lh.shape[1], rh.shape[1] // 2
    width = both // 2
    lh[size:, :], ll[size:, :] = split(values)
    f_at, t_at = columns(both, half_width)
    for left, right in ((lh, rh), (ll, rl)):
        for lanes, at in ((slice(0, half_width), f_at), (slice(half_width, 2 * half_width), t_at)):
            right[:size, lanes] = left[size:, at]
            right[size:, lanes] = left[:size, at]
    cross = dot3((lh[:, :width], ll[:, :width]), (rh[...], rl[...]), TN)
    close = dot3((lh[:, width:], ll[:, width:]), (rh[:, half_width:], rl[:, half_width:]), TN)
    return cross, close


def update_kernel(cap, n, k, *refs):
    arrivals = arrivals_of(n)
    fresh = k == 1
    if fresh:
        own, refs = refs[0], refs[1:]
    else:
        (old_v, old_ab, old_ee, old_image, own), refs = refs[:5], refs[5:]
    up, down = refs[:2], refs[2:4]
    v_next, ab, ee, image, blk, middle, fth, ftl, kh, kl, lh, ll, rh, rl = refs[4:]
    both, half_width = fth.shape[1], ee.shape[1]
    news = ([0] if fresh else []) + [2 * k - 1, 2 * k]
    later = news[-1] + 1
    size = cap * len(news)
    if fresh:
        blk[:cap, :both] = own[:, :both]
    base = len(news) - 2
    assemble(cap, up, blk, base)
    assemble(cap, down, blk, base + 1)
    middle[...] = jnp.zeros(middle.shape, F32)
    kh[...] = jnp.zeros(kh.shape, BF16)
    kl[...] = jnp.zeros(kl.shape, BF16)
    for a, x in enumerate(news):
        rows = slice(a * cap, (a + 1) * cap)
        for y in range(x, n):
            if x == 0:
                value = own[:, both + y * cap : both + (y + 1) * cap]
            else:
                way = -1 if arrivals[x] < 0 else 1
                slot = (way * (arrivals[y] - arrivals[x])) % n
                if slot >= n - 2 * k + (1 if way < 0 or slot == 0 else 0):
                    continue
                value = blk[rows, both + slot * cap : both + (slot + 1) * cap]
            if y in news:
                b = news.index(y)
                middle[rows, b * cap : (b + 1) * cap] = value * 0.5 if y == x else value
            else:
                lanes = slice((y - later) * LANES, (y - later) * LANES + cap)
                kh[rows, lanes], kl[rows, lanes] = split(value)
    sh, sl = split(blk[:, :both])
    fth[...], ftl[...] = sh, sl
    lh[:size, :], ll[:size, :] = sh, sl
    values = dot3(split(middle[...]), (sh, sl), NN)
    if not fresh:
        values = values + jnp.concatenate([old_v[:cap, :], old_v[LANES : LANES + cap, :]], axis=0)
    cross, close = pairs(size, values, lh, ll, rh, rl)
    to_come = dot3((kh[...], kl[...]), (sh, sl), TN)
    part = split(own[:, both + news[0] * cap : both + later * cap])
    f_at, t_at = columns(both, half_width)
    image_f = dot3(part, (fth[:, f_at], ftl[:, f_at]), NN)
    image_t = dot3(part, (fth[:, t_at], ftl[:, t_at]), NN)
    if fresh:
        ab[...], ee[...], v_next[...] = cross, close, to_come
        image[:, :half_width], image[:, half_width:] = image_f, image_t
    else:
        ab[...] = old_ab[...] + cross
        ee[...] = old_ee[...] + close
        v_next[...] = old_v[2 * LANES :, :] + to_come
        image[:, :half_width] = old_image[:, :half_width] + image_f
        image[:, half_width:] = old_image[:, half_width:] + image_t


def last_kernel(cap, n, up, down, up_far, down_far, old_v, old_ab, old_ee, image, own, code, m2, corner1, corner2, cross0, diag0, *refs):
    c1, g1, c2, xx, g2, flat, flat_far, blk, lh, ll, rh, rl, c1_v, g1_v, c2_v, xx_v, g2_v, corner1_v, corner2_v, cross0_v, diag0_v, sems = refs
    row, col = lax.axis_index("row"), lax.axis_index("col")
    both, half_width = lh.shape[1], old_ee.shape[1]
    half_at = pl.ds(pl.multiple_of(col * half_width, half_width), half_width)
    loads = [
        pltpu.make_async_copy(corner1.at[:, half_at], corner1_v, sems.at[5]),
        pltpu.make_async_copy(corner2, corner2_v, sems.at[6]),
        pltpu.make_async_copy(cross0, cross0_v, sems.at[7]),
        pltpu.make_async_copy(diag0, diag0_v, sems.at[8]),
    ]
    for load in loads:
        load.start()
    cut = up.shape[0]
    flat[:cut, :], flat[cut:, :] = up[...], down[...]
    flat_far[:cut, :], flat_far[cut:, :] = up_far[...], down_far[...]
    assemble(cap, (flat, flat_far), blk, 0)
    sh, sl = split(blk[:, :both])
    lh[:cap, :], ll[:cap, :] = sh, sl
    values = dot3(split(blk[:, both : both + cap] * 0.5), (sh, sl), NN) + old_v[:cap, :]
    cross, close = pairs(cap, values, lh, ll, rh, rl)
    for load in loads:
        load.wait()
    copies = []

    def send(value, ref, out):
        ref[...] = value
        copies.append(pltpu.make_async_copy(ref, out, sems.at[len(copies)]))
        copies[-1].start()

    send(corner1_v[...] + (old_ab[:, :half_width] + cross[:, :half_width]), g1_v, g1)
    send(old_ab[:, half_width:] + cross[:, half_width:] - cross0_v[...], xx_v, xx)
    send(corner2_v[...] + (diag0_v[...] + (old_ee[...] + close)), g2_v, g2)
    k = split(own[:, both + (n - 1) * cap :])
    pick = picker(code[pl.ds(row, 1), :], cap)
    pick2 = (pick.astype(F32) * m2[pl.ds(row, 1), :]).astype(BF16)
    f_at, t_at = columns(both, half_width)
    image_f = image[:, :half_width] + dot3(k, (lh[:cap, f_at], ll[:cap, f_at]), NN)
    send(-dot2(pick, split(image_f), TN), c1_v, c1)
    image_t = image[:, half_width:] + dot3(k, (lh[:cap, t_at], ll[:cap, t_at]), NN)
    send(-dot2(pick2, split(image_t), TN), c2_v, c2)
    for copy in copies:
        copy.wait()


def call_factors(cap, n, anc1, anc2, first_factor, second_factor, second_link):
    block, width = first_factor.shape
    return pl.pallas_call(
        functools.partial(factors_kernel, cap, n),
        out_shape=(
            jax.ShapeDtypeStruct((cap, 2 * width), F32),
            jax.ShapeDtypeStruct((n, block), jnp.int32),
            jax.ShapeDtypeStruct((n, block), F32),
            jax.ShapeDtypeStruct((1, LANES), F32),
        ),
        in_specs=[ANY] * 5,
        out_specs=(VMEM,) * 4,
        scratch_shapes=[pltpu.VMEM(v.shape, v.dtype) for v in (anc1, anc2, first_factor, second_factor, second_link)] + [pltpu.SemaphoreType.DMA((5,))],
        cost_estimate=pl.CostEstimate(flops=6 * cap * width * width, bytes_accessed=4 * width * (2 * block + width), transcendentals=0),
        name="factors",
    )(anc1, anc2, first_factor, second_factor, second_link)


def call_payload(cap, n, code, factors, mine, theirs):
    _, _, block = mine.shape
    both, half = factors.shape[1], cap // 2
    counts = (n - 1, n - 2)
    flats = [jax.ShapeDtypeStruct(((both // LANES + chunks_of(count * cap)) * half, LANES), F32) for count in counts]
    return pl.pallas_call(
        functools.partial(payload_kernel, cap, n, counts),
        out_shape=(jax.ShapeDtypeStruct((cap, both + n * cap), F32), *flats),
        in_specs=[VMEM, VMEM, ANY, VMEM],
        out_specs=(VMEM,) * 3,
        scratch_shapes=[
            pltpu.VMEM((n * block, block), F32),
            pltpu.VMEM((cap, n * block), F32),
            pltpu.VMEM((2, cap, chunks_of(counts[0] * cap) * LANES), F32),
            pltpu.VMEM((n * cap, block), BF16),
            pltpu.VMEM(mine.shape, F32),
            pltpu.SemaphoreType.DMA((1,)),
        ],
        cost_estimate=pl.CostEstimate(flops=8 * cap * block * n * block, bytes_accessed=8 * n * block * block, transcendentals=0),
        name="payload",
    )(code, factors, mine, theirs)


def gather_branch(cap, n, code, m2, own, own_up, own_down, second_link, first_corner, second_corner):
    block = code.shape[1]
    width = second_link.shape[0]
    half_width = second_corner.shape[1]
    half, both = cap // 2, 2 * width
    square = jax.ShapeDtypeStruct((width, half_width), F32)
    tall = jax.ShapeDtypeStruct((block, half_width), F32)

    order = [*range(0, n, 2), *range(n - 1, 0, -2)]
    ups = [(order[k], order[(k + 1) % n]) for k in range(n)]
    downs = [(b, a) for a, b in ups]
    swap = [(0, 1), (1, 0)]

    def scratch_of(blocks):
        size = cap * blocks
        return [
            pltpu.VMEM((2 * size, both), BF16),
            pltpu.VMEM((2 * size, both), BF16),
            pltpu.VMEM((2 * size, 2 * half_width), BF16),
            pltpu.VMEM((2 * size, 2 * half_width), BF16),
        ]

    params = pltpu.CompilerParams(vmem_limit_bytes=40 << 20)
    cross0, diag0 = pl.pallas_call(
        side_kernel,
        out_shape=(square, square),
        in_specs=[VMEM] * 2,
        out_specs=(VMEM, VMEM),
        scratch_shapes=[pltpu.VMEM((width, half_width), F32)],
        cost_estimate=pl.CostEstimate(flops=12 * width * width * half_width, bytes_accessed=20 * width * width, transcendentals=0),
        name="side",
    )(first_corner, second_link)

    def flat_rows(count):
        return (both // LANES + chunks_of(count * cap)) * half

    up, down = own_up, own_down
    state = ()
    for k in range(1, n // 2):
        up = lax.ppermute(up[: flat_rows(n + 1 - 2 * k)], "row", ups)
        down = lax.ppermute(down[: flat_rows(n - 2 * k)], "row", downs)
        up_far, down_far = lax.ppermute(up, "col", swap), lax.ppermute(down, "col", swap)
        blocks = 3 if k == 1 else 2
        size = blocks * cap
        later = (n - 1 - 2 * k) * LANES
        ins = [*state, own, up, up_far, down, down_far]
        outs = [jax.ShapeDtypeStruct(shape, F32) for shape in ((later, both), (width, 2 * half_width), (width, half_width), (cap, 2 * half_width))]
        state = pl.pallas_call(
            functools.partial(update_kernel, cap, n, k),
            out_shape=tuple(outs),
            in_specs=[VMEM] * len(ins),
            out_specs=(VMEM,) * len(outs),
            scratch_shapes=[
                pltpu.VMEM((size, both + chunks_of((n - 1) * cap) * LANES), F32),
                pltpu.VMEM((size, size), F32),
                pltpu.VMEM((size, both), BF16),
                pltpu.VMEM((size, both), BF16),
                pltpu.VMEM((size, later), BF16),
                pltpu.VMEM((size, later), BF16),
            ]
            + scratch_of(blocks),
            compiler_params=params,
            cost_estimate=pl.CostEstimate(flops=6 * size * width * (2 * size + 2 * later + 6 * half_width), bytes_accessed=4 * size * width * 8, transcendentals=0),
        )(*ins)
    rows = flat_rows(1)
    cut = 3 * rows // 40 * 8
    k = n // 2
    up = lax.ppermute(up[:cut], "row", ups)
    down = lax.ppermute(down[cut:rows], "row", downs)
    up_far, down_far = lax.ppermute(up, "col", swap), lax.ppermute(down, "col", swap)
    return pl.pallas_call(
        functools.partial(last_kernel, cap, n),
        out_shape=(tall, square, tall, square, square),
        in_specs=[VMEM] * 11 + [ANY] * 4,
        out_specs=(ANY,) * 5,
        scratch_shapes=[pltpu.VMEM((rows, LANES), F32)] * 2
        + [pltpu.VMEM((cap, both + chunks_of(cap) * LANES), F32)]
        + scratch_of(1)
        + [pltpu.VMEM(shape.shape, F32) for shape in (tall, square, tall, square, square)]
        + [pltpu.VMEM(square.shape, F32)] * 4
        + [pltpu.SemaphoreType.DMA((9,))],
        compiler_params=params,
        cost_estimate=pl.CostEstimate(flops=6 * cap * width * (2 * width + 6 * half_width), bytes_accessed=4 * width * width * 5, transcendentals=0),
        name="last",
    )(up, down, up_far, down_far, *state, own, code, m2, first_corner, second_corner, cross0, diag0)


def gather_plan(n, known_inverse, first_factor, first_corner, first_ancestors, second_factor, second_link, second_corner, second_ancestors):
    _, _, block = known_inverse.shape
    theirs = lax.ppermute(known_inverse, "col", [(0, 1), (1, 0)])
    anc1, anc2 = first_ancestors[None, :], second_ancestors[None, :]
    mean = -(-first_ancestors.shape[0] // n)
    cap = min(-(-mean * 5 // 64) * 16, block)
    factors, code, m2, most = call_factors(cap, n, anc1, anc2, first_factor, second_factor, second_link)
    own = call_payload(cap, n, code, factors, known_inverse, theirs)

    def compact(own, code, m2, known_inverse, theirs, anc1, anc2, first_factor, second_factor, second_link, first_corner, second_corner):
        return gather_branch(cap, n, code, m2, *own, second_link, first_corner, second_corner)

    def general(own, code, m2, known_inverse, theirs, anc1, anc2, first_factor, second_factor, second_link, first_corner, second_corner):
        factors, code, m2, _ = call_factors(block, n, anc1, anc2, first_factor, second_factor, second_link)
        own = call_payload(block, n, code, factors, known_inverse, theirs)
        return gather_branch(block, n, code, m2, *own, second_link, first_corner, second_corner)

    operands = (own, code, m2, known_inverse, theirs, anc1, anc2, first_factor, second_factor, second_link, first_corner, second_corner)
    if cap == block:
        return compact(*operands)
    return lax.cond(most[0, 0] <= cap, compact, general, *operands)


def solution(mesh):
    n = mesh.shape["row"]

    def on_device(known_inverse, *rest):
        _, _, block = known_inverse.shape
        width = rest[0].shape[1]
        if n % 2 == 0 and n > 4 and block % LANES == 0 and mesh.shape["col"] == 2 and (n * block) ** 2 <= 12 * width**2:
            return gather_plan(n, known_inverse, *rest)
        return reduce_plan(known_inverse, *rest)

    return jax.shard_map(
        on_device,
        mesh=mesh,
        in_specs=(
            P("pole", "col", "row"),
            P(("pole", "row"), None),
            P("pole", None),
            P("pole"),
            P(("pole", "row"), None),
            P("pole", None),
            P("pole", "col"),
            P("pole"),
        ),
        out_specs=(
            P(("pole", "row"), "col"),
            P("pole", "col"),
            P(("pole", "row"), "col"),
            P("pole", "col"),
            P("pole", "col"),
        ),
        check_vma=False,
    )
```

```python
import functools

import jax
import jax.numpy as jnp
from jax import lax
from jax.experimental import pallas as pl
from jax.experimental.pallas import tpu as pltpu
from jax.sharding import PartitionSpec as P


HIGH = lax.Precision.HIGHEST
F32, BF16 = jnp.float32, jnp.bfloat16
LANES = 128
UNIT = 256
NN = (((1,), (0,)), ((), ()))
NT = (((1,), (1,)), ((), ()))
TN = (((0,), (0,)), ((), ()))
VMEM = pl.BlockSpec(memory_space=pltpu.VMEM)
SMEM = pl.BlockSpec(memory_space=pltpu.SMEM)
ANY = pl.BlockSpec(memory_space=pl.ANY)


def product(left, right):
    return jnp.dot(left, right, precision=HIGH, preferred_element_type=F32)


def transposed_product(left, right):
    return lax.dot_general(left, right, TN, precision=HIGH, preferred_element_type=F32)


def mask_of(ancestors, row_start, rows):
    numbers = row_start + jnp.arange(rows, dtype=jnp.int32)
    return jnp.any(ancestors[:, None] == numbers[None, :], axis=0).astype(F32)


def reduce_plan(known_inverse, first_factor, first_corner, first_ancestors, second_factor, second_link, second_corner, second_ancestors):
    groups, share_rows, block_rows = known_inverse.shape
    half_width = second_corner.shape[1]
    col_index = lax.axis_index("col")
    row_start = lax.axis_index("row") * block_rows
    first_mask = mask_of(first_ancestors, row_start, block_rows)[:, None]
    second_mask = mask_of(second_ancestors, row_start, block_rows)[:, None]
    first_masked = first_factor * first_mask
    second_masked = second_factor * second_mask
    share_start = col_index * share_rows
    first_piece = lax.dynamic_slice_in_dim(first_masked, share_start, share_rows, 0)
    second_piece = lax.dynamic_slice_in_dim(second_masked, share_start, share_rows, 0)
    columns = known_inverse.reshape(groups * share_rows, block_rows)
    first_partial = transposed_product(columns, lax.all_gather(first_piece, "row", axis=0, tiled=True))
    second_partial = transposed_product(columns, lax.all_gather(second_piece, "row", axis=0, tiled=True))
    first_image = lax.psum_scatter(first_partial, "col", scatter_dimension=1, tiled=True)
    first_column = -(first_image * first_mask)
    first_full = lax.all_gather(first_column, "col", axis=1, tiled=True)
    diagonal_partial = transposed_product(first_masked, first_column)
    corner_half = lax.dynamic_slice_in_dim(first_corner, col_index * half_width, half_width, 1)
    first_diagonal = corner_half - lax.psum(diagonal_partial, "row")
    diagonal_full = lax.all_gather(first_diagonal, "col", axis=1, tiled=True)
    second_image = lax.psum_scatter(second_partial, "col", scatter_dimension=1, tiled=True)
    link_half = lax.dynamic_slice_in_dim(second_link, col_index * half_width, half_width, 1)
    second_column = -((second_image + product(first_full, link_half)) * second_mask)
    second_half = lax.dynamic_slice_in_dim(second_masked, col_index * half_width, half_width, 1)
    cross_partial = transposed_product(first_full, second_half)
    closing_partial = transposed_product(second_masked, second_column)
    cross_total, closing_total = lax.psum((cross_partial, closing_partial), "row")
    second_cross = -(cross_total + product(diagonal_full, link_half))
    second_diagonal = second_corner - closing_total - transposed_product(second_link, second_cross)
    return (first_column, first_diagonal, second_column, second_cross, second_diagonal)


def dot(left, right, dims):
    return lax.dot_general(left, right, dims, preferred_element_type=F32)


def split(value):
    high = value.astype(BF16)
    return high, (value - high.astype(F32)).astype(BF16)


def passes(lefts, rights, dims):
    (left_axis,), (right_axis,) = dims[0]
    depth, count = lefts[0].shape[left_axis], len(lefts)
    if -(-count * depth // UNIT) < count * -(-depth // UNIT):
        return dot(jnp.concatenate(lefts, axis=left_axis), jnp.concatenate(rights, axis=right_axis), dims)
    total = None
    for left, right in zip(lefts, rights):
        value = dot(left, right, dims)
        total = value if total is None else total + value
    return total


def dot3(left, right, dims):
    (lh, ll), (rh, rl) = left, right
    return passes([lh, ll, lh], [rl, rh, rh], dims)


def dot2(exact, right, dims, flip=False):
    rh, rl = right
    if flip:
        return passes([rl, rh], [exact, exact], dims)
    return passes([exact, exact], [rl, rh], dims)


def slot_codes(mask):
    block = mask.shape[1]
    before = (lax.broadcasted_iota(jnp.int32, (block, block), 0) < lax.broadcasted_iota(jnp.int32, (block, block), 1)).astype(BF16)
    rank = dot(mask.astype(BF16), before, NN)
    return jnp.where(mask > 0, rank, -1.0).astype(jnp.int32)


def marks(ancestors, n, block):
    count = ancestors.shape[1]
    group = lax.div(ancestors, block)
    inside = ancestors - group * block
    groups = (lax.broadcasted_iota(jnp.int32, (n, count), 0) == group).astype(BF16)
    insides = (lax.broadcasted_iota(jnp.int32, (block, count), 0) == inside).astype(BF16)
    return dot(groups, insides, NT)


def picker(code_row, slots, offset=0):
    block = code_row.shape[1]
    at = lax.broadcasted_iota(jnp.int32, (slots, block), 0) - offset
    return ((at == code_row) & (code_row >= 0)).astype(BF16)


def rows_at(start, size, step=8):
    return pl.ds(pl.multiple_of(start, step), size)


def fetch(pairs, sems):
    copies = [pltpu.make_async_copy(source, target, sems.at[k]) for k, (source, target) in enumerate(pairs)]
    for copy in copies:
        copy.start()
    return copies


def factors_kernel(caps, n, anc1_h, anc2_h, first_h, second_h, first_c, second_c, code1, code2, over, anc1, anc2, first, second, sems):
    loads = fetch(((anc1_h, anc1), (anc2_h, anc2), (first_h, first), (second_h, second)), sems)
    row = lax.axis_index("row")
    block = first.shape[0]
    excess = jnp.zeros((1, 1), F32)
    for load, ancestors, code, cap in zip(loads, (anc1, anc2), (code1, code2), caps):
        load.wait()
        mask = marks(ancestors[...], n, block)
        code[...] = slot_codes(mask)
        excess = jnp.maximum(excess, jnp.max(jnp.sum(mask, axis=1, keepdims=True), axis=0, keepdims=True) - cap)
    over[...] = jnp.broadcast_to(excess, over.shape)
    for load, source, code, cap, out in zip(loads[2:], (first, second), (code1, code2), caps, (first_c, second_c)):
        pick = picker(code[pl.ds(row, 1), :], cap)
        load.wait()
        out[...] = dot2(pick, split(source[...]), NN)


def place_of(row, n):
    return jnp.where(lax.rem(row, 2) == 0, lax.div(row, 2), n - 1 - lax.div(row, 2))


def row_of(place, n):
    return jnp.where(place < n // 2, 2 * place, 2 * (n - 1 - place) + 1)


def chunks_of(lanes):
    return -(-lanes // LANES)


def arrivals_of(n):
    return [0] + [sign * k for k in range(1, n // 2) for sign in (-1, 1)] + [n // 2]


def payload_kernel(caps, n, counts, code, first_c, second_c, mine_h, theirs, own, up, down, cols, images, own_ud, spreads, mine, sems):
    loads = fetch(((mine_h, mine),), sems)
    row, col = lax.axis_index("row"), lax.axis_index("col")
    groups, share, block = mine.shape
    cap, width = caps[0], first_c.shape[1]
    half, half2 = caps[0] // 2, caps[1] // 2
    for g in range(groups):
        cols[rows_at(g * block + (1 - col) * share, share), :] = theirs[g]
        spreads[g * cap : (g + 1) * cap, :] = picker(code[g : g + 1, :], cap)
    own_ud[...] = jnp.zeros(own_ud.shape, F32)
    pick = picker(code[pl.ds(row, 1), :], cap)
    loads[0].wait()
    for g in range(groups):
        cols[rows_at(g * block + col * share, share), :] = mine[g]
    images[...] = dot2(pick, split(cols[...]), NT)
    arrivals = arrivals_of(n)
    place = place_of(row, n)
    for d in range(n):
        g = row_of(lax.rem(place + d, n), n)
        spread = spreads[rows_at(g * cap, cap, 16), :]
        image = images[:, pl.ds(pl.multiple_of(g * block, block), block)]
        value = dot2(spread, split(image), NT, flip=True)
        x = arrivals.index(d if d <= n // 2 else d - n)
        own[:, width + x * cap : width + (x + 1) * cap] = value
        for way, slot in ((0, (n - d) % n), (1, d)):
            if slot < counts[way]:
                own_ud[way, :, slot * cap : (slot + 1) * cap] = value
    own[:, :width] = first_c[...]
    mine_rows, mine_rows2 = rows_at(col * half, half), rows_at(col * half2, half2)
    for way, out in ((0, up), (1, down)):
        at = 0
        for c in range(width // LANES):
            out[at : at + half, :] = first_c[mine_rows, c * LANES : (c + 1) * LANES]
            at += half
        for c in range(width // LANES):
            out[at : at + half2, :] = second_c[mine_rows2, c * LANES : (c + 1) * LANES]
            at += half2
        for c in range(chunks_of(counts[way] * cap)):
            out[at : at + half, :] = own_ud[way, mine_rows, c * LANES : (c + 1) * LANES]
            at += half


def side_kernel(corner, link, cross0, diag0, link_h, link_l, link_half):
    half_width = cross0.shape[1]
    start = pl.multiple_of(lax.axis_index("col") * half_width, half_width)
    link_half[...] = link[:, pl.ds(start, half_width)]
    link_h[...], link_l[...] = split(link[...])
    value = dot3(split(corner[...]), split(link_half[...]), NN)
    cross0[...] = value
    diag0[...] = dot3((link_h[...], link_l[...]), split(value), TN)


def assemble(caps, width, flat, blk, sblk, k):
    col = lax.axis_index("col")
    half, half2 = caps[0] // 2, caps[1] // 2
    for value, side in zip(flat, (col, 1 - col)):
        rows, rows2 = rows_at(k * caps[0] + side * half, half), rows_at(k * caps[1] + side * half2, half2)
        at = 0
        for c in range(width // LANES):
            blk[rows, c * LANES : (c + 1) * LANES] = value[at : at + half, :]
            at += half
        for c in range(width // LANES):
            sblk[rows2, c * LANES : (c + 1) * LANES] = value[at : at + half2, :]
            at += half2
        for c in range((value.shape[0] - at) // half):
            blk[rows, width + c * LANES : width + (c + 1) * LANES] = value[at : at + half, :]
            at += half


def source_row(distance, n):
    return row_of(lax.rem(place_of(lax.axis_index("row"), n) + distance + n, n), n)


def factors_of(caps, n, distances, blk, sblk, code1, code2, link, lh, ll):
    cap, cap2 = caps
    width = link[0].shape[0]
    size = cap * len(distances)
    first = split(blk[:, :width])
    lh[:size, :width], ll[:size, :width] = first
    image = dot3(first, (link[0][...], link[1][...]), NN)
    for k, distance in enumerate(distances):
        g = source_row(distance, n)
        spread = dot(picker(code1[pl.ds(g, 1), :], cap), picker(code2[pl.ds(g, 1), :], cap2), NT).astype(BF16)
        rows = slice(k * cap, (k + 1) * cap)
        second = dot2(spread, split(sblk[k * cap2 : (k + 1) * cap2, :]), NN)
        lh[rows, width:], ll[rows, width:] = split(second - image[rows, :])


def columns(both, half_width):
    start = lax.axis_index("col") * half_width
    f_at = pl.ds(pl.multiple_of(start, half_width), half_width)
    t_at = pl.ds(pl.multiple_of(both // 2 + start, half_width), half_width)
    return f_at, t_at


def pairs(size, values, lh, ll, rh, rl):
    both, half_width = lh.shape[1], rh.shape[1] // 2
    width = both // 2
    lh[size:, :], ll[size:, :] = split(values)
    f_at, t_at = columns(both, half_width)
    for left, right in ((lh, rh), (ll, rl)):
        for lanes, at in ((slice(0, half_width), f_at), (slice(half_width, 2 * half_width), t_at)):
            right[:size, lanes] = left[size:, at]
            right[size:, lanes] = left[:size, at]
    cross = dot3((lh[:, :width], ll[:, :width]), (rh[...], rl[...]), TN)
    close = dot3((lh[:, width:], ll[:, width:]), (rh[:, half_width:], rl[:, half_width:]), TN)
    return cross, close


def update_kernel(caps, n, k, *refs):
    arrivals = arrivals_of(n)
    fresh = k == 1
    cap = caps[0]
    (own, code1, code2, link_h, link_l), refs = refs[:5], refs[5:]
    if fresh:
        own_s, refs = refs[0], refs[1:]
    else:
        (old_v, old_ab, old_ee, old_image), refs = refs[:4], refs[4:]
    up, down = refs[:2], refs[2:4]
    v_next, ab, ee, image, blk, sblk, middle, kh, kl, lh, ll, rh, rl = refs[4:]
    both, half_width = lh.shape[1], ee.shape[1]
    width = both // 2
    news = ([0] if fresh else []) + [2 * k - 1, 2 * k]
    later = news[-1] + 1
    size = cap * len(news)
    if fresh:
        blk[:cap, :width] = own[:, :width]
        sblk[: caps[1], :] = own_s[...]
    base = len(news) - 2
    assemble(caps, width, up, blk, sblk, base)
    assemble(caps, width, down, blk, sblk, base + 1)
    factors_of(caps, n, [arrivals[x] for x in news], blk, sblk, code1, code2, (link_h, link_l), lh, ll)
    middle[...] = jnp.zeros(middle.shape, F32)
    kh[...] = jnp.zeros(kh.shape, BF16)
    kl[...] = jnp.zeros(kl.shape, BF16)
    for a, x in enumerate(news):
        rows = slice(a * cap, (a + 1) * cap)
        for y in range(x, n):
            if x == 0:
                value = own[:, width + y * cap : width + (y + 1) * cap]
            else:
                way = -1 if arrivals[x] < 0 else 1
                slot = (way * (arrivals[y] - arrivals[x])) % n
                if slot >= n - 2 * k + (1 if way < 0 or slot == 0 else 0):
                    continue
                value = blk[rows, width + slot * cap : width + (slot + 1) * cap]
            if y in news:
                b = news.index(y)
                middle[rows, b * cap : (b + 1) * cap] = value * 0.5 if y == x else value
            else:
                lanes = slice((y - later) * LANES, (y - later) * LANES + cap)
                kh[rows, lanes], kl[rows, lanes] = split(value)
    sh, sl = lh[:size, :], ll[:size, :]
    values = dot3(split(middle[...]), (sh, sl), NN)
    if not fresh:
        values = values + jnp.concatenate([old_v[:cap, :], old_v[LANES : LANES + cap, :]], axis=0)
    cross, close = pairs(size, values, lh, ll, rh, rl)
    to_come = dot3((kh[...], kl[...]), (sh, sl), TN)
    part = split(own[:, width + news[0] * cap : width + later * cap])
    f_at, t_at = columns(both, half_width)
    image_f = dot3(part, (lh[:size, f_at], ll[:size, f_at]), NN)
    image_t = dot3(part, (lh[:size, t_at], ll[:size, t_at]), NN)
    if fresh:
        ab[...], ee[...], v_next[...] = cross, close, to_come
        image[:, :half_width], image[:, half_width:] = image_f, image_t
    else:
        ab[...] = old_ab[...] + cross
        ee[...] = old_ee[...] + close
        v_next[...] = old_v[2 * LANES :, :] + to_come
        image[:, :half_width] = old_image[:, :half_width] + image_f
        image[:, half_width:] = old_image[:, half_width:] + image_t


def last_kernel(caps, n, up, down, up_far, down_far, old_v, old_ab, old_ee, image, own, code1, code2, link_h, link_l, corner1, corner2, cross0, diag0, *refs):
    cap = caps[0]
    c1, g1, c2, xx, g2, flat, flat_far, blk, sblk, lh, ll, rh, rl, c1_v, g1_v, c2_v, xx_v, g2_v, corner1_v, corner2_v, cross0_v, diag0_v, sems = refs
    row, col = lax.axis_index("row"), lax.axis_index("col")
    both, half_width = lh.shape[1], old_ee.shape[1]
    half_at = pl.ds(pl.multiple_of(col * half_width, half_width), half_width)
    loads = [
        pltpu.make_async_copy(corner1.at[:, half_at], corner1_v, sems.at[5]),
        pltpu.make_async_copy(corner2, corner2_v, sems.at[6]),
        pltpu.make_async_copy(cross0, cross0_v, sems.at[7]),
        pltpu.make_async_copy(diag0, diag0_v, sems.at[8]),
    ]
    for load in loads:
        load.start()
    cut = up.shape[0]
    flat[:cut, :], flat[cut:, :] = up[...], down[...]
    flat_far[:cut, :], flat_far[cut:, :] = up_far[...], down_far[...]
    width = both // 2
    assemble(caps, width, (flat, flat_far), blk, sblk, 0)
    factors_of(caps, n, [n // 2], blk, sblk, code1, code2, (link_h, link_l), lh, ll)
    values = dot3(split(blk[:, width : width + cap] * 0.5), (lh[:cap, :], ll[:cap, :]), NN) + old_v[:cap, :]
    cross, close = pairs(cap, values, lh, ll, rh, rl)
    for load in loads:
        load.wait()
    copies = []

    def send(value, ref, out):
        ref[...] = value
        copies.append(pltpu.make_async_copy(ref, out, sems.at[len(copies)]))
        copies[-1].start()

    send(corner1_v[...] + (old_ab[:, :half_width] + cross[:, :half_width]), g1_v, g1)
    send(old_ab[:, half_width:] + cross[:, half_width:] - cross0_v[...], xx_v, xx)
    send(corner2_v[...] + (diag0_v[...] + (old_ee[...] + close)), g2_v, g2)
    k = split(own[:, width + (n - 1) * cap :])
    pick = picker(code1[pl.ds(row, 1), :], cap)
    pick2 = (pick.astype(F32) * (code2[pl.ds(row, 1), :] >= 0).astype(F32)).astype(BF16)
    f_at, t_at = columns(both, half_width)
    image_f = image[:, :half_width] + dot3(k, (lh[:cap, f_at], ll[:cap, f_at]), NN)
    send(-dot2(pick, split(image_f), TN), c1_v, c1)
    image_t = image[:, half_width:] + dot3(k, (lh[:cap, t_at], ll[:cap, t_at]), NN)
    send(-dot2(pick2, split(image_t), TN), c2_v, c2)
    for copy in copies:
        copy.wait()


def call_factors(caps, n, anc1, anc2, first_factor, second_factor):
    block, width = first_factor.shape
    codes = jax.ShapeDtypeStruct((n, block), jnp.int32)
    return pl.pallas_call(
        functools.partial(factors_kernel, caps, n),
        out_shape=(
            jax.ShapeDtypeStruct((caps[0], width), F32),
            jax.ShapeDtypeStruct((caps[1], width), F32),
            codes,
            codes,
            jax.ShapeDtypeStruct((1, LANES), F32),
        ),
        in_specs=[ANY] * 4,
        out_specs=(VMEM,) * 5,
        scratch_shapes=[pltpu.VMEM(v.shape, v.dtype) for v in (anc1, anc2, first_factor, second_factor)] + [pltpu.SemaphoreType.DMA((4,))],
        cost_estimate=pl.CostEstimate(flops=8 * sum(caps) * block * width, bytes_accessed=8 * width * block, transcendentals=0),
        name="factors",
    )(anc1, anc2, first_factor, second_factor)


def call_payload(caps, n, code, first_c, second_c, mine, theirs):
    _, _, block = mine.shape
    cap, width = first_c.shape
    counts = (n - 1, n - 2)
    flats = [jax.ShapeDtypeStruct((flat_rows(caps, width, count), LANES), F32) for count in counts]
    return pl.pallas_call(
        functools.partial(payload_kernel, caps, n, counts),
        out_shape=(jax.ShapeDtypeStruct((cap, width + n * cap), F32), *flats),
        in_specs=[VMEM, VMEM, VMEM, ANY, VMEM],
        out_specs=(VMEM,) * 3,
        scratch_shapes=[
            pltpu.VMEM((n * block, block), F32),
            pltpu.VMEM((cap, n * block), F32),
            pltpu.VMEM((2, cap, chunks_of(counts[0] * cap) * LANES), F32),
            pltpu.VMEM((n * cap, block), BF16),
            pltpu.VMEM(mine.shape, F32),
            pltpu.SemaphoreType.DMA((1,)),
        ],
        cost_estimate=pl.CostEstimate(flops=8 * cap * block * n * block, bytes_accessed=8 * n * block * block, transcendentals=0),
        name="payload",
    )(code, first_c, second_c, mine, theirs)


def flat_rows(caps, width, count):
    return width // LANES * (caps[0] // 2 + caps[1] // 2) + chunks_of(count * caps[0]) * (caps[0] // 2)


def gather_branch(caps, n, code1, code2, second_c, own, own_up, own_down, second_link, first_corner, second_corner):
    cap = caps[0]
    block = code1.shape[1]
    width = second_link.shape[0]
    half_width = second_corner.shape[1]
    both = 2 * width
    square = jax.ShapeDtypeStruct((width, half_width), F32)
    tall = jax.ShapeDtypeStruct((block, half_width), F32)

    order = [*range(0, n, 2), *range(n - 1, 0, -2)]
    ups = [(order[k], order[(k + 1) % n]) for k in range(n)]
    downs = [(b, a) for a, b in ups]
    swap = [(0, 1), (1, 0)]

    def scratch_of(blocks):
        size = cap * blocks
        return [
            pltpu.VMEM((2 * size, both), BF16),
            pltpu.VMEM((2 * size, both), BF16),
            pltpu.VMEM((2 * size, 2 * half_width), BF16),
            pltpu.VMEM((2 * size, 2 * half_width), BF16),
        ]

    params = pltpu.CompilerParams(vmem_limit_bytes=40 << 20)
    part = pltpu.VMEM((width, width), BF16)
    cross0, diag0, link_h, link_l = pl.pallas_call(
        side_kernel,
        out_shape=(square, square, part, part),
        in_specs=[VMEM] * 2,
        out_specs=(VMEM,) * 4,
        scratch_shapes=[pltpu.VMEM((width, half_width), F32)],
        cost_estimate=pl.CostEstimate(flops=12 * width * width * half_width, bytes_accessed=20 * width * width, transcendentals=0),
        name="side",
    )(first_corner, second_link)

    up, down = own_up, own_down
    state = ()
    for k in range(1, n // 2):
        up = lax.ppermute(up[: flat_rows(caps, width, n + 1 - 2 * k)], "row", ups)
        down = lax.ppermute(down[: flat_rows(caps, width, n - 2 * k)], "row", downs)
        up_far, down_far = lax.ppermute(up, "col", swap), lax.ppermute(down, "col", swap)
        blocks = 3 if k == 1 else 2
        size = blocks * cap
        later = (n - 1 - 2 * k) * LANES
        ins = [own, code1, code2, link_h, link_l, *(state or (second_c,)), up, up_far, down, down_far]
        outs = [jax.ShapeDtypeStruct(shape, F32) for shape in ((later, both), (width, 2 * half_width), (width, half_width), (cap, 2 * half_width))]
        state = pl.pallas_call(
            functools.partial(update_kernel, caps, n, k),
            out_shape=tuple(outs),
            in_specs=[VMEM] * len(ins),
            out_specs=(VMEM,) * len(outs),
            scratch_shapes=[
                pltpu.VMEM((size, width + chunks_of((n - 1) * cap) * LANES), F32),
                pltpu.VMEM((blocks * caps[1], width), F32),
                pltpu.VMEM((size, size), F32),
                pltpu.VMEM((size, later), BF16),
                pltpu.VMEM((size, later), BF16),
            ]
            + scratch_of(blocks),
            compiler_params=params,
            cost_estimate=pl.CostEstimate(flops=6 * size * width * (2 * size + 2 * later + 6 * half_width), bytes_accessed=4 * size * width * 8, transcendentals=0),
        )(*ins)
    rows = flat_rows(caps, width, 1)
    cut = 3 * rows // 40 * 8
    k = n // 2
    up = lax.ppermute(up[:cut], "row", ups)
    down = lax.ppermute(down[cut:rows], "row", downs)
    up_far, down_far = lax.ppermute(up, "col", swap), lax.ppermute(down, "col", swap)
    return pl.pallas_call(
        functools.partial(last_kernel, caps, n),
        out_shape=(tall, square, tall, square, square),
        in_specs=[VMEM] * 13 + [ANY] * 4,
        out_specs=(ANY,) * 5,
        scratch_shapes=[pltpu.VMEM((rows, LANES), F32)] * 2
        + [pltpu.VMEM((cap, width + chunks_of(cap) * LANES), F32), pltpu.VMEM((caps[1], width), F32)]
        + scratch_of(1)
        + [pltpu.VMEM(shape.shape, F32) for shape in (tall, square, tall, square, square)]
        + [pltpu.VMEM(square.shape, F32)] * 4
        + [pltpu.SemaphoreType.DMA((9,))],
        compiler_params=params,
        cost_estimate=pl.CostEstimate(flops=6 * cap * width * (2 * width + 6 * half_width), bytes_accessed=4 * width * width * 5, transcendentals=0),
        name="last",
    )(up, down, up_far, down_far, *state, own, code1, code2, link_h, link_l, first_corner, second_corner, cross0, diag0)


def gather_plan(n, known_inverse, first_factor, first_corner, first_ancestors, second_factor, second_link, second_corner, second_ancestors):
    _, _, block = known_inverse.shape
    theirs = lax.ppermute(known_inverse, "col", [(0, 1), (1, 0)])
    anc1, anc2 = first_ancestors[None, :], second_ancestors[None, :]
    mean1, mean2 = -(-first_ancestors.shape[0] // n), -(-second_ancestors.shape[0] // n)
    caps = (min(-(-mean1 * 5 // 64) * 16, block), min(-(-mean2 * 3 // 32) * 16, block))
    first_c, second_c, code1, code2, over = call_factors(caps, n, anc1, anc2, first_factor, second_factor)
    own = call_payload(caps, n, code1, first_c, second_c, known_inverse, theirs)

    def compact(own, second_c, code1, code2, known_inverse, theirs, anc1, anc2, first_factor, second_factor, second_link, first_corner, second_corner):
        return gather_branch(caps, n, code1, code2, second_c, *own, second_link, first_corner, second_corner)

    def general(own, second_c, code1, code2, known_inverse, theirs, anc1, anc2, first_factor, second_factor, second_link, first_corner, second_corner):
        every = (block, block)
        first_c, second_c, code1, code2, _ = call_factors(every, n, anc1, anc2, first_factor, second_factor)
        own = call_payload(every, n, code1, first_c, second_c, known_inverse, theirs)
        return gather_branch(every, n, code1, code2, second_c, *own, second_link, first_corner, second_corner)

    operands = (own, second_c, code1, code2, known_inverse, theirs, anc1, anc2, first_factor, second_factor, second_link, first_corner, second_corner)
    if caps == (block, block):
        return compact(*operands)
    return lax.cond(over[0, 0] <= 0, compact, general, *operands)


def solution(mesh):
    n = mesh.shape["row"]

    def on_device(known_inverse, *rest):
        _, _, block = known_inverse.shape
        width = rest[0].shape[1]
        if n % 2 == 0 and n > 4 and block % LANES == 0 and mesh.shape["col"] == 2 and (n * block) ** 2 <= 12 * width**2:
            return gather_plan(n, known_inverse, *rest)
        return reduce_plan(known_inverse, *rest)

    return jax.shard_map(
        on_device,
        mesh=mesh,
        in_specs=(
            P("pole", "col", "row"),
            P(("pole", "row"), None),
            P("pole", None),
            P("pole"),
            P(("pole", "row"), None),
            P("pole", None),
            P("pole", "col"),
            P("pole"),
        ),
        out_specs=(
            P(("pole", "row"), "col"),
            P("pole", "col"),
            P(("pole", "row"), "col"),
            P("pole", "col"),
            P("pole", "col"),
        ),
        check_vma=False,
    )
```

```python
import functools

import jax
import jax.numpy as jnp
from jax import lax
from jax.experimental import pallas as pl
from jax.experimental.pallas import tpu as pltpu
from jax.sharding import PartitionSpec as P


HIGH = lax.Precision.HIGHEST
F32, BF16 = jnp.float32, jnp.bfloat16
LANES = 128
UNIT = 256
NN = (((1,), (0,)), ((), ()))
NT = (((1,), (1,)), ((), ()))
TN = (((0,), (0,)), ((), ()))
VMEM = pl.BlockSpec(memory_space=pltpu.VMEM)
SMEM = pl.BlockSpec(memory_space=pltpu.SMEM)
ANY = pl.BlockSpec(memory_space=pl.ANY)


def product(left, right):
    return jnp.dot(left, right, precision=HIGH, preferred_element_type=F32)


def transposed_product(left, right):
    return lax.dot_general(left, right, TN, precision=HIGH, preferred_element_type=F32)


def mask_of(ancestors, row_start, rows):
    numbers = row_start + jnp.arange(rows, dtype=jnp.int32)
    return jnp.any(ancestors[:, None] == numbers[None, :], axis=0).astype(F32)


def reduce_plan(known_inverse, first_factor, first_corner, first_ancestors, second_factor, second_link, second_corner, second_ancestors):
    groups, share_rows, block_rows = known_inverse.shape
    half_width = second_corner.shape[1]
    col_index = lax.axis_index("col")
    row_start = lax.axis_index("row") * block_rows
    first_mask = mask_of(first_ancestors, row_start, block_rows)[:, None]
    second_mask = mask_of(second_ancestors, row_start, block_rows)[:, None]
    first_masked = first_factor * first_mask
    second_masked = second_factor * second_mask
    share_start = col_index * share_rows
    first_piece = lax.dynamic_slice_in_dim(first_masked, share_start, share_rows, 0)
    second_piece = lax.dynamic_slice_in_dim(second_masked, share_start, share_rows, 0)
    columns = known_inverse.reshape(groups * share_rows, block_rows)
    first_partial = transposed_product(columns, lax.all_gather(first_piece, "row", axis=0, tiled=True))
    second_partial = transposed_product(columns, lax.all_gather(second_piece, "row", axis=0, tiled=True))
    first_image = lax.psum_scatter(first_partial, "col", scatter_dimension=1, tiled=True)
    first_column = -(first_image * first_mask)
    first_full = lax.all_gather(first_column, "col", axis=1, tiled=True)
    diagonal_partial = transposed_product(first_masked, first_column)
    corner_half = lax.dynamic_slice_in_dim(first_corner, col_index * half_width, half_width, 1)
    first_diagonal = corner_half - lax.psum(diagonal_partial, "row")
    diagonal_full = lax.all_gather(first_diagonal, "col", axis=1, tiled=True)
    second_image = lax.psum_scatter(second_partial, "col", scatter_dimension=1, tiled=True)
    link_half = lax.dynamic_slice_in_dim(second_link, col_index * half_width, half_width, 1)
    second_column = -((second_image + product(first_full, link_half)) * second_mask)
    second_half = lax.dynamic_slice_in_dim(second_masked, col_index * half_width, half_width, 1)
    cross_partial = transposed_product(first_full, second_half)
    closing_partial = transposed_product(second_masked, second_column)
    cross_total, closing_total = lax.psum((cross_partial, closing_partial), "row")
    second_cross = -(cross_total + product(diagonal_full, link_half))
    second_diagonal = second_corner - closing_total - transposed_product(second_link, second_cross)
    return (first_column, first_diagonal, second_column, second_cross, second_diagonal)


def dot(left, right, dims):
    return lax.dot_general(left, right, dims, preferred_element_type=F32)


def split(value):
    high = value.astype(BF16)
    return high, (value - high.astype(F32)).astype(BF16)


def passes(lefts, rights, dims):
    (left_axis,), (right_axis,) = dims[0]
    depth, count = lefts[0].shape[left_axis], len(lefts)
    if -(-count * depth // UNIT) < count * -(-depth // UNIT):
        return dot(jnp.concatenate(lefts, axis=left_axis), jnp.concatenate(rights, axis=right_axis), dims)
    total = None
    for left, right in zip(lefts, rights):
        value = dot(left, right, dims)
        total = value if total is None else total + value
    return total


def dot3(left, right, dims):
    (lh, ll), (rh, rl) = left, right
    return passes([lh, ll, lh], [rl, rh, rh], dims)


def dot2(exact, right, dims, flip=False):
    rh, rl = right
    if flip:
        return passes([rl, rh], [exact, exact], dims)
    return passes([exact, exact], [rl, rh], dims)


def slot_codes(mask):
    block = mask.shape[1]
    before = (lax.broadcasted_iota(jnp.int32, (block, block), 0) < lax.broadcasted_iota(jnp.int32, (block, block), 1)).astype(BF16)
    rank = dot(mask.astype(BF16), before, NN)
    return jnp.where(mask > 0, rank, -1.0).astype(jnp.int32)


def marks(ancestors, n, block):
    count = ancestors.shape[1]
    group = lax.div(ancestors, block)
    inside = ancestors - group * block
    groups = (lax.broadcasted_iota(jnp.int32, (n, count), 0) == group).astype(BF16)
    insides = (lax.broadcasted_iota(jnp.int32, (block, count), 0) == inside).astype(BF16)
    return dot(groups, insides, NT)


def picker(code_row, slots, offset=0):
    block = code_row.shape[1]
    at = lax.broadcasted_iota(jnp.int32, (slots, block), 0) - offset
    return ((at == code_row) & (code_row >= 0)).astype(BF16)


def rows_at(start, size, step=8):
    return pl.ds(pl.multiple_of(start, step), size)


def fetch(pairs, sems):
    copies = [pltpu.make_async_copy(source, target, sems.at[k]) for k, (source, target) in enumerate(pairs)]
    for copy in copies:
        copy.start()
    return copies


def factors_kernel(caps, n, anc1_h, anc2_h, first_h, second_h, first_c, second_c, code1, code2, over, anc1, anc2, first, second, sems):
    loads = fetch(((anc1_h, anc1), (anc2_h, anc2), (first_h, first), (second_h, second)), sems)
    row = lax.axis_index("row")
    block = first.shape[0]
    excess = jnp.zeros((1, 1), F32)
    for load, ancestors, code, cap in zip(loads, (anc1, anc2), (code1, code2), caps):
        load.wait()
        mask = marks(ancestors[...], n, block)
        code[...] = slot_codes(mask)
        excess = jnp.maximum(excess, jnp.max(jnp.sum(mask, axis=1, keepdims=True), axis=0, keepdims=True) - cap)
    over[0, 0] = excess[0, 0].astype(jnp.int32)
    for load, source, code, cap, out in zip(loads[2:], (first, second), (code1, code2), caps, (first_c, second_c)):
        pick = picker(code[pl.ds(row, 1), :], cap)
        load.wait()
        out[...] = dot2(pick, split(source[...]), NN)


def place_of(row, n):
    return jnp.where(lax.rem(row, 2) == 0, lax.div(row, 2), n - 1 - lax.div(row, 2))


def row_of(place, n):
    return jnp.where(place < n // 2, 2 * place, 2 * (n - 1 - place) + 1)


def chunks_of(lanes):
    return -(-lanes // LANES)


def arrivals_of(n):
    return [0] + [sign * k for k in range(1, n // 2) for sign in (-1, 1)] + [n // 2]


def payload_kernel(caps, n, counts, code, first_c, second_c, mine_h, theirs, own, up, down, cols, images, own_ud, spreads, mine, sems):
    loads = fetch(((mine_h, mine),), sems)
    row, col = lax.axis_index("row"), lax.axis_index("col")
    groups, share, block = mine.shape
    cap, width = caps[0], first_c.shape[1]
    half, half2 = caps[0] // 2, caps[1] // 2
    for g in range(groups):
        cols[rows_at(g * block + (1 - col) * share, share), :] = theirs[g]
        spreads[g * cap : (g + 1) * cap, :] = picker(code[g : g + 1, :], cap)
    own_ud[...] = jnp.zeros(own_ud.shape, F32)
    pick = picker(code[pl.ds(row, 1), :], cap)
    loads[0].wait()
    for g in range(groups):
        cols[rows_at(g * block + col * share, share), :] = mine[g]
    images[...] = dot2(pick, split(cols[...]), NT)
    arrivals = arrivals_of(n)
    place = place_of(row, n)
    values = []
    for d in range(n):
        g = row_of(lax.rem(place + d, n), n)
        spread = spreads[rows_at(g * cap, cap, 16), :]
        image = images[:, pl.ds(pl.multiple_of(g * block, block), block)]
        values.append(dot2(spread, split(image), NT, flip=True))
    for d, value in enumerate(values):
        x = arrivals.index(d if d <= n // 2 else d - n)
        own[:, width + x * cap : width + (x + 1) * cap] = value
        for way, slot in ((0, (n - d) % n), (1, d)):
            if slot < counts[way]:
                own_ud[way, :, slot * cap : (slot + 1) * cap] = value
    own[:, :width] = first_c[...]
    mine_rows, mine_rows2 = rows_at(col * half, half), rows_at(col * half2, half2)
    for way, out in ((0, up), (1, down)):
        at = 0
        for c in range(width // LANES):
            out[at : at + half, :] = first_c[mine_rows, c * LANES : (c + 1) * LANES]
            at += half
        for c in range(width // LANES):
            out[at : at + half2, :] = second_c[mine_rows2, c * LANES : (c + 1) * LANES]
            at += half2
        for c in range(chunks_of(counts[way] * cap)):
            out[at : at + half, :] = own_ud[way, mine_rows, c * LANES : (c + 1) * LANES]
            at += half


def side_kernel(corner, link, cross0, diag0, link_h, link_l, link_half):
    half_width = cross0.shape[1]
    start = pl.multiple_of(lax.axis_index("col") * half_width, half_width)
    link_half[...] = link[:, pl.ds(start, half_width)]
    link_h[...], link_l[...] = split(link[...])
    value = dot3(split(corner[...]), split(link_half[...]), NN)
    cross0[...] = value
    diag0[...] = dot3((link_h[...], link_l[...]), split(value), TN)


def assemble(caps, width, flat, blk, sblk, k):
    col = lax.axis_index("col")
    half, half2 = caps[0] // 2, caps[1] // 2
    for value, side in zip(flat, (col, 1 - col)):
        rows, rows2 = rows_at(k * caps[0] + side * half, half), rows_at(k * caps[1] + side * half2, half2)
        at = 0
        for c in range(width // LANES):
            blk[rows, c * LANES : (c + 1) * LANES] = value[at : at + half, :]
            at += half
        for c in range(width // LANES):
            sblk[rows2, c * LANES : (c + 1) * LANES] = value[at : at + half2, :]
            at += half2
        for c in range((value.shape[0] - at) // half):
            blk[rows, width + c * LANES : width + (c + 1) * LANES] = value[at : at + half, :]
            at += half


def source_row(distance, n):
    return row_of(lax.rem(place_of(lax.axis_index("row"), n) + distance + n, n), n)


def factors_of(caps, n, distances, blk, sblk, code1, code2, link, lh, ll):
    cap, cap2 = caps
    width = link[0].shape[0]
    size = cap * len(distances)
    first = split(blk[:, :width])
    lh[:size, :width], ll[:size, :width] = first
    image = dot3(first, (link[0][...], link[1][...]), NN)
    for k, distance in enumerate(distances):
        g = source_row(distance, n)
        spread = dot(picker(code1[pl.ds(g, 1), :], cap), picker(code2[pl.ds(g, 1), :], cap2), NT).astype(BF16)
        rows = slice(k * cap, (k + 1) * cap)
        second = dot2(spread, split(sblk[k * cap2 : (k + 1) * cap2, :]), NN)
        lh[rows, width:], ll[rows, width:] = split(second - image[rows, :])


def columns(both, half_width):
    start = lax.axis_index("col") * half_width
    f_at = pl.ds(pl.multiple_of(start, half_width), half_width)
    t_at = pl.ds(pl.multiple_of(both // 2 + start, half_width), half_width)
    return f_at, t_at


def pairs(size, values, lh, ll, rh, rl):
    both, half_width = lh.shape[1], rh.shape[1] // 2
    width = both // 2
    lh[size:, :], ll[size:, :] = split(values)
    f_at, t_at = columns(both, half_width)
    for left, right in ((lh, rh), (ll, rl)):
        for lanes, at in ((slice(0, half_width), f_at), (slice(half_width, 2 * half_width), t_at)):
            right[:size, lanes] = left[size:, at]
            right[size:, lanes] = left[:size, at]
    cross = dot3((lh[:, :width], ll[:, :width]), (rh[...], rl[...]), TN)
    close = dot3((lh[:, width:], ll[:, width:]), (rh[:, half_width:], rl[:, half_width:]), TN)
    return cross, close


def update_kernel(caps, n, k, *refs):
    arrivals = arrivals_of(n)
    fresh = k == 1
    cap = caps[0]
    (own, code1, code2, link_h, link_l), refs = refs[:5], refs[5:]
    if fresh:
        own_s, refs = refs[0], refs[1:]
    else:
        (old_v, old_ab, old_ee, old_image), refs = refs[:4], refs[4:]
    up, down = refs[:2], refs[2:4]
    v_next, ab, ee, image, blk, sblk, middle, kh, kl, lh, ll, rh, rl = refs[4:]
    both, half_width = lh.shape[1], ee.shape[1]
    width = both // 2
    news = ([0] if fresh else []) + [2 * k - 1, 2 * k]
    later = news[-1] + 1
    size = cap * len(news)
    if fresh:
        blk[:cap, :width] = own[:, :width]
        sblk[: caps[1], :] = own_s[...]
    base = len(news) - 2
    assemble(caps, width, up, blk, sblk, base)
    assemble(caps, width, down, blk, sblk, base + 1)
    factors_of(caps, n, [arrivals[x] for x in news], blk, sblk, code1, code2, (link_h, link_l), lh, ll)
    middle[...] = jnp.zeros(middle.shape, F32)
    kh[...] = jnp.zeros(kh.shape, BF16)
    kl[...] = jnp.zeros(kl.shape, BF16)
    for a, x in enumerate(news):
        rows = slice(a * cap, (a + 1) * cap)
        for y in range(x, n):
            if x == 0:
                value = own[:, width + y * cap : width + (y + 1) * cap]
            else:
                way = -1 if arrivals[x] < 0 else 1
                slot = (way * (arrivals[y] - arrivals[x])) % n
                if slot >= n - 2 * k + (1 if way < 0 or slot == 0 else 0):
                    continue
                value = blk[rows, width + slot * cap : width + (slot + 1) * cap]
            if y in news:
                b = news.index(y)
                middle[rows, b * cap : (b + 1) * cap] = value * 0.5 if y == x else value
            else:
                lanes = slice((y - later) * LANES, (y - later) * LANES + cap)
                kh[rows, lanes], kl[rows, lanes] = split(value)
    sh, sl = lh[:size, :], ll[:size, :]
    values = dot3(split(middle[...]), (sh, sl), NN)
    if not fresh:
        values = values + jnp.concatenate([old_v[:cap, :], old_v[LANES : LANES + cap, :]], axis=0)
    cross, close = pairs(size, values, lh, ll, rh, rl)
    to_come = dot3((kh[...], kl[...]), (sh, sl), TN)
    part = split(own[:, width + news[0] * cap : width + later * cap])
    f_at, t_at = columns(both, half_width)
    image_f = dot3(part, (lh[:size, f_at], ll[:size, f_at]), NN)
    image_t = dot3(part, (lh[:size, t_at], ll[:size, t_at]), NN)
    if fresh:
        ab[...], ee[...], v_next[...] = cross, close, to_come
        image[:, :half_width], image[:, half_width:] = image_f, image_t
    else:
        ab[...] = old_ab[...] + cross
        ee[...] = old_ee[...] + close
        v_next[...] = old_v[2 * LANES :, :] + to_come
        image[:, :half_width] = old_image[:, :half_width] + image_f
        image[:, half_width:] = old_image[:, half_width:] + image_t


def last_kernel(caps, n, up, down, up_far, down_far, old_v, old_ab, old_ee, image, own, code1, code2, link_h, link_l, corner1, corner2, cross0, diag0, *refs):
    cap = caps[0]
    c1, g1, c2, xx, g2, flat, flat_far, blk, sblk, lh, ll, rh, rl, c1_v, g1_v, c2_v, xx_v, g2_v, corner1_v, corner2_v, cross0_v, diag0_v, sems = refs
    row, col = lax.axis_index("row"), lax.axis_index("col")
    both, half_width = lh.shape[1], old_ee.shape[1]
    half_at = pl.ds(pl.multiple_of(col * half_width, half_width), half_width)
    loads = [
        pltpu.make_async_copy(corner1.at[:, half_at], corner1_v, sems.at[5]),
        pltpu.make_async_copy(corner2, corner2_v, sems.at[6]),
        pltpu.make_async_copy(cross0, cross0_v, sems.at[7]),
        pltpu.make_async_copy(diag0, diag0_v, sems.at[8]),
    ]
    for load in loads:
        load.start()
    cut = up.shape[0]
    flat[:cut, :], flat[cut:, :] = up[...], down[...]
    flat_far[:cut, :], flat_far[cut:, :] = up_far[...], down_far[...]
    width = both // 2
    assemble(caps, width, (flat, flat_far), blk, sblk, 0)
    factors_of(caps, n, [n // 2], blk, sblk, code1, code2, (link_h, link_l), lh, ll)
    values = dot3(split(blk[:, width : width + cap] * 0.5), (lh[:cap, :], ll[:cap, :]), NN) + old_v[:cap, :]
    cross, close = pairs(cap, values, lh, ll, rh, rl)
    for load in loads:
        load.wait()
    copies = []

    def send(value, ref, out):
        ref[...] = value
        copies.append(pltpu.make_async_copy(ref, out, sems.at[len(copies)]))
        copies[-1].start()

    send(corner1_v[...] + (old_ab[:, :half_width] + cross[:, :half_width]), g1_v, g1)
    send(old_ab[:, half_width:] + cross[:, half_width:] - cross0_v[...], xx_v, xx)
    send(corner2_v[...] + (diag0_v[...] + (old_ee[...] + close)), g2_v, g2)
    k = split(own[:, width + (n - 1) * cap :])
    pick = picker(code1[pl.ds(row, 1), :], cap)
    pick2 = (pick.astype(F32) * (code2[pl.ds(row, 1), :] >= 0).astype(F32)).astype(BF16)
    f_at, t_at = columns(both, half_width)
    image_f = image[:, :half_width] + dot3(k, (lh[:cap, f_at], ll[:cap, f_at]), NN)
    send(-dot2(pick, split(image_f), TN), c1_v, c1)
    image_t = image[:, half_width:] + dot3(k, (lh[:cap, t_at], ll[:cap, t_at]), NN)
    send(-dot2(pick2, split(image_t), TN), c2_v, c2)
    for copy in copies:
        copy.wait()


def call_factors(caps, n, anc1, anc2, first_factor, second_factor):
    block, width = first_factor.shape
    codes = pltpu.VMEM((n, block), jnp.int32)
    return pl.pallas_call(
        functools.partial(factors_kernel, caps, n),
        out_shape=(
            pltpu.VMEM((caps[0], width), F32),
            pltpu.VMEM((caps[1], width), F32),
            codes,
            codes,
            pltpu.SMEM((1, 1), jnp.int32),
        ),
        in_specs=[ANY] * 4,
        out_specs=(VMEM,) * 4 + (SMEM,),
        scratch_shapes=[pltpu.VMEM(v.shape, v.dtype) for v in (anc1, anc2, first_factor, second_factor)] + [pltpu.SemaphoreType.DMA((4,))],
        cost_estimate=pl.CostEstimate(flops=8 * sum(caps) * block * width, bytes_accessed=8 * width * block, transcendentals=0),
        name="factors",
    )(anc1, anc2, first_factor, second_factor)


def call_payload(caps, n, code, first_c, second_c, mine, theirs):
    _, _, block = mine.shape
    cap, width = first_c.shape
    counts = (n - 1, n - 2)
    flats = [jax.ShapeDtypeStruct((flat_rows(caps, width, count), LANES), F32) for count in counts]
    return pl.pallas_call(
        functools.partial(payload_kernel, caps, n, counts),
        out_shape=(jax.ShapeDtypeStruct((cap, width + n * cap), F32), *flats),
        in_specs=[VMEM, VMEM, VMEM, ANY, VMEM],
        out_specs=(VMEM,) * 3,
        scratch_shapes=[
            pltpu.VMEM((n * block, block), F32),
            pltpu.VMEM((cap, n * block), F32),
            pltpu.VMEM((2, cap, chunks_of(counts[0] * cap) * LANES), F32),
            pltpu.VMEM((n * cap, block), BF16),
            pltpu.VMEM(mine.shape, F32),
            pltpu.SemaphoreType.DMA((1,)),
        ],
        cost_estimate=pl.CostEstimate(flops=8 * cap * block * n * block, bytes_accessed=8 * n * block * block, transcendentals=0),
        name="payload",
    )(code, pltpu.with_memory_space_constraint(first_c, pltpu.VMEM), second_c, mine, theirs)


def flat_rows(caps, width, count):
    return width // LANES * (caps[0] // 2 + caps[1] // 2) + chunks_of(count * caps[0]) * (caps[0] // 2)


def gather_branch(caps, n, code1, code2, second_c, own, own_up, own_down, second_link, first_corner, second_corner):
    cap = caps[0]
    block = code1.shape[1]
    width = second_link.shape[0]
    half_width = second_corner.shape[1]
    both = 2 * width
    square = jax.ShapeDtypeStruct((width, half_width), F32)
    tall = jax.ShapeDtypeStruct((block, half_width), F32)

    order = [*range(0, n, 2), *range(n - 1, 0, -2)]
    ups = [(order[k], order[(k + 1) % n]) for k in range(n)]
    downs = [(b, a) for a, b in ups]
    swap = [(0, 1), (1, 0)]

    def scratch_of(blocks):
        size = cap * blocks
        return [
            pltpu.VMEM((2 * size, both), BF16),
            pltpu.VMEM((2 * size, both), BF16),
            pltpu.VMEM((2 * size, 2 * half_width), BF16),
            pltpu.VMEM((2 * size, 2 * half_width), BF16),
        ]

    params = pltpu.CompilerParams(vmem_limit_bytes=40 << 20)
    part = pltpu.VMEM((width, width), BF16)
    cross0, diag0, link_h, link_l = pl.pallas_call(
        side_kernel,
        out_shape=(square, square, part, part),
        in_specs=[VMEM] * 2,
        out_specs=(VMEM,) * 4,
        scratch_shapes=[pltpu.VMEM((width, half_width), F32)],
        cost_estimate=pl.CostEstimate(flops=12 * width * width * half_width, bytes_accessed=20 * width * width, transcendentals=0),
        name="side",
    )(first_corner, second_link)

    up, down = own_up, own_down
    state = ()
    for k in range(1, n // 2):
        up = lax.ppermute(up[: flat_rows(caps, width, n + 1 - 2 * k)], "row", ups)
        down = lax.ppermute(down[: flat_rows(caps, width, n - 2 * k)], "row", downs)
        up_far, down_far = lax.ppermute(up, "col", swap), lax.ppermute(down, "col", swap)
        blocks = 3 if k == 1 else 2
        size = blocks * cap
        later = (n - 1 - 2 * k) * LANES
        ins = [own, code1, code2, link_h, link_l, *(state or (second_c,)), up, up_far, down, down_far]
        outs = [jax.ShapeDtypeStruct(shape, F32) for shape in ((later, both), (width, 2 * half_width), (width, half_width), (cap, 2 * half_width))]
        state = pl.pallas_call(
            functools.partial(update_kernel, caps, n, k),
            out_shape=tuple(outs),
            in_specs=[VMEM] * len(ins),
            out_specs=(VMEM,) * len(outs),
            scratch_shapes=[
                pltpu.VMEM((size, width + chunks_of((n - 1) * cap) * LANES), F32),
                pltpu.VMEM((blocks * caps[1], width), F32),
                pltpu.VMEM((size, size), F32),
                pltpu.VMEM((size, later), BF16),
                pltpu.VMEM((size, later), BF16),
            ]
            + scratch_of(blocks),
            compiler_params=params,
            cost_estimate=pl.CostEstimate(flops=6 * size * width * (2 * size + 2 * later + 6 * half_width), bytes_accessed=4 * size * width * 8, transcendentals=0),
        )(*ins)
    rows = flat_rows(caps, width, 1)
    cut = 7 * rows // 80 * 8
    k = n // 2
    up = lax.ppermute(up[:cut], "row", ups)
    down = lax.ppermute(down[cut:rows], "row", downs)
    up_far, down_far = lax.ppermute(up, "col", swap), lax.ppermute(down, "col", swap)
    return pl.pallas_call(
        functools.partial(last_kernel, caps, n),
        out_shape=(tall, square, tall, square, square),
        in_specs=[VMEM] * 13 + [ANY] * 4,
        out_specs=(ANY,) * 5,
        scratch_shapes=[pltpu.VMEM((rows, LANES), F32)] * 2
        + [pltpu.VMEM((cap, width + chunks_of(cap) * LANES), F32), pltpu.VMEM((caps[1], width), F32)]
        + scratch_of(1)
        + [pltpu.VMEM(shape.shape, F32) for shape in (tall, square, tall, square, square)]
        + [pltpu.VMEM(square.shape, F32)] * 4
        + [pltpu.SemaphoreType.DMA((9,))],
        compiler_params=params,
        cost_estimate=pl.CostEstimate(flops=6 * cap * width * (2 * width + 6 * half_width), bytes_accessed=4 * width * width * 5, transcendentals=0),
        name="last",
    )(up, down, up_far, down_far, *state, own, code1, code2, link_h, link_l, first_corner, second_corner, cross0, diag0)


def gather_plan(n, known_inverse, first_factor, first_corner, first_ancestors, second_factor, second_link, second_corner, second_ancestors):
    _, _, block = known_inverse.shape
    theirs = lax.ppermute(known_inverse, "col", [(0, 1), (1, 0)])
    anc1, anc2 = first_ancestors[None, :], second_ancestors[None, :]
    mean1, mean2 = -(-first_ancestors.shape[0] // n), -(-second_ancestors.shape[0] // n)
    caps = (min(-(-mean1 * 5 // 64) * 16, block), min(-(-mean2 * 3 // 32) * 16, block))
    first_c, second_c, code1, code2, over = call_factors(caps, n, anc1, anc2, first_factor, second_factor)
    own = call_payload(caps, n, code1, first_c, second_c, known_inverse, theirs)

    def compact(own, second_c, code1, code2, known_inverse, theirs, anc1, anc2, first_factor, second_factor, second_link, first_corner, second_corner):
        return gather_branch(caps, n, code1, code2, second_c, *own, second_link, first_corner, second_corner)

    def general(own, second_c, code1, code2, known_inverse, theirs, anc1, anc2, first_factor, second_factor, second_link, first_corner, second_corner):
        every = (block, block)
        first_c, second_c, code1, code2, _ = call_factors(every, n, anc1, anc2, first_factor, second_factor)
        own = call_payload(every, n, code1, first_c, second_c, known_inverse, theirs)
        return gather_branch(every, n, code1, code2, second_c, *own, second_link, first_corner, second_corner)

    operands = (own, second_c, code1, code2, known_inverse, theirs, anc1, anc2, first_factor, second_factor, second_link, first_corner, second_corner)
    if caps == (block, block):
        return compact(*operands)
    return lax.cond(over[0, 0] <= 0, compact, general, *operands)


def solution(mesh):
    n = mesh.shape["row"]

    def on_device(known_inverse, *rest):
        _, _, block = known_inverse.shape
        width = rest[0].shape[1]
        if n % 2 == 0 and n > 4 and block % LANES == 0 and mesh.shape["col"] == 2 and (n * block) ** 2 <= 12 * width**2:
            return gather_plan(n, known_inverse, *rest)
        return reduce_plan(known_inverse, *rest)

    return jax.shard_map(
        on_device,
        mesh=mesh,
        in_specs=(
            P("pole", "col", "row"),
            P(("pole", "row"), None),
            P("pole", None),
            P("pole"),
            P(("pole", "row"), None),
            P("pole", None),
            P("pole", "col"),
            P("pole"),
        ),
        out_specs=(
            P(("pole", "row"), "col"),
            P("pole", "col"),
            P(("pole", "row"), "col"),
            P("pole", "col"),
            P("pole", "col"),
        ),
        check_vma=False,
    )
```

```python
import functools

import jax
import jax.numpy as jnp
from jax import lax
from jax.experimental import pallas as pl
from jax.experimental.pallas import tpu as pltpu
from jax.sharding import PartitionSpec as P


HIGH = lax.Precision.HIGHEST
F32, BF16 = jnp.float32, jnp.bfloat16
LANES = 128
UNIT = 256
NN = (((1,), (0,)), ((), ()))
NT = (((1,), (1,)), ((), ()))
TN = (((0,), (0,)), ((), ()))
VMEM = pl.BlockSpec(memory_space=pltpu.VMEM)
SMEM = pl.BlockSpec(memory_space=pltpu.SMEM)
ANY = pl.BlockSpec(memory_space=pl.ANY)


def product(left, right):
    return jnp.dot(left, right, precision=HIGH, preferred_element_type=F32)


def transposed_product(left, right):
    return lax.dot_general(left, right, TN, precision=HIGH, preferred_element_type=F32)


def mask_of(ancestors, row_start, rows):
    numbers = row_start + jnp.arange(rows, dtype=jnp.int32)
    return jnp.any(ancestors[:, None] == numbers[None, :], axis=0).astype(F32)


def reduce_plan(known_inverse, first_factor, first_corner, first_ancestors, second_factor, second_link, second_corner, second_ancestors):
    groups, share_rows, block_rows = known_inverse.shape
    half_width = second_corner.shape[1]
    col_index = lax.axis_index("col")
    row_start = lax.axis_index("row") * block_rows
    first_mask = mask_of(first_ancestors, row_start, block_rows)[:, None]
    second_mask = mask_of(second_ancestors, row_start, block_rows)[:, None]
    first_masked = first_factor * first_mask
    second_masked = second_factor * second_mask
    share_start = col_index * share_rows
    first_piece = lax.dynamic_slice_in_dim(first_masked, share_start, share_rows, 0)
    second_piece = lax.dynamic_slice_in_dim(second_masked, share_start, share_rows, 0)
    columns = known_inverse.reshape(groups * share_rows, block_rows)
    first_partial = transposed_product(columns, lax.all_gather(first_piece, "row", axis=0, tiled=True))
    second_partial = transposed_product(columns, lax.all_gather(second_piece, "row", axis=0, tiled=True))
    first_image = lax.psum_scatter(first_partial, "col", scatter_dimension=1, tiled=True)
    first_column = -(first_image * first_mask)
    first_full = lax.all_gather(first_column, "col", axis=1, tiled=True)
    diagonal_partial = transposed_product(first_masked, first_column)
    corner_half = lax.dynamic_slice_in_dim(first_corner, col_index * half_width, half_width, 1)
    first_diagonal = corner_half - lax.psum(diagonal_partial, "row")
    diagonal_full = lax.all_gather(first_diagonal, "col", axis=1, tiled=True)
    second_image = lax.psum_scatter(second_partial, "col", scatter_dimension=1, tiled=True)
    link_half = lax.dynamic_slice_in_dim(second_link, col_index * half_width, half_width, 1)
    second_column = -((second_image + product(first_full, link_half)) * second_mask)
    second_half = lax.dynamic_slice_in_dim(second_masked, col_index * half_width, half_width, 1)
    cross_partial = transposed_product(first_full, second_half)
    closing_partial = transposed_product(second_masked, second_column)
    cross_total, closing_total = lax.psum((cross_partial, closing_partial), "row")
    second_cross = -(cross_total + product(diagonal_full, link_half))
    second_diagonal = second_corner - closing_total - transposed_product(second_link, second_cross)
    return (first_column, first_diagonal, second_column, second_cross, second_diagonal)


def dot(left, right, dims):
    return lax.dot_general(left, right, dims, preferred_element_type=F32)


def split(value):
    high = value.astype(BF16)
    return high, (value - high.astype(F32)).astype(BF16)


def passes(lefts, rights, dims):
    (left_axis,), (right_axis,) = dims[0]
    depth, count = lefts[0].shape[left_axis], len(lefts)
    if -(-count * depth // UNIT) < count * -(-depth // UNIT):
        return dot(jnp.concatenate(lefts, axis=left_axis), jnp.concatenate(rights, axis=right_axis), dims)
    total = None
    for left, right in zip(lefts, rights):
        value = dot(left, right, dims)
        total = value if total is None else total + value
    return total


def dot3(left, right, dims):
    (lh, ll), (rh, rl) = left, right
    return passes([lh, ll, lh], [rl, rh, rh], dims)


def dot2(exact, right, dims, flip=False):
    rh, rl = right
    if flip:
        return passes([rl, rh], [exact, exact], dims)
    return passes([exact, exact], [rl, rh], dims)


def slot_codes(mask):
    block = mask.shape[1]
    before = (lax.broadcasted_iota(jnp.int32, (block, block), 0) < lax.broadcasted_iota(jnp.int32, (block, block), 1)).astype(BF16)
    rank = dot(mask.astype(BF16), before, NN)
    return jnp.where(mask > 0, rank, -1.0).astype(jnp.int32)


def marks(ancestors, n, block):
    count = ancestors.shape[1]
    group = lax.div(ancestors, block)
    inside = ancestors - group * block
    groups = (lax.broadcasted_iota(jnp.int32, (n, count), 0) == group).astype(BF16)
    insides = (lax.broadcasted_iota(jnp.int32, (block, count), 0) == inside).astype(BF16)
    return dot(groups, insides, NT)


def picker(code_row, slots, offset=0):
    block = code_row.shape[1]
    at = lax.broadcasted_iota(jnp.int32, (slots, block), 0) - offset
    return ((at == code_row) & (code_row >= 0)).astype(BF16)


def rows_at(start, size, step=8):
    return pl.ds(pl.multiple_of(start, step), size)


def fetch(pairs, sems):
    copies = [pltpu.make_async_copy(source, target, sems.at[k]) for k, (source, target) in enumerate(pairs)]
    for copy in copies:
        copy.start()
    return copies


def factors_kernel(caps, n, anc1_h, anc2_h, first_h, second_h, first_c, second_c, code1, code2, over, anc1, anc2, first, second, sems):
    loads = fetch(((anc1_h, anc1), (anc2_h, anc2), (first_h, first), (second_h, second)), sems)
    row = lax.axis_index("row")
    block = first.shape[0]
    excess = jnp.zeros((1, 1), F32)
    for load, ancestors, code, cap in zip(loads, (anc1, anc2), (code1, code2), caps):
        load.wait()
        mask = marks(ancestors[...], n, block)
        code[...] = slot_codes(mask)
        excess = jnp.maximum(excess, jnp.max(jnp.sum(mask, axis=1, keepdims=True), axis=0, keepdims=True) - cap)
    over[0, 0] = excess[0, 0].astype(jnp.int32)
    for load, source, code, cap, out in zip(loads[2:], (first, second), (code1, code2), caps, (first_c, second_c)):
        pick = picker(code[pl.ds(row, 1), :], cap)
        load.wait()
        out[...] = dot2(pick, split(source[...]), NN)


def place_of(row, n):
    return jnp.where(lax.rem(row, 2) == 0, lax.div(row, 2), n - 1 - lax.div(row, 2))


def row_of(place, n):
    return jnp.where(place < n // 2, 2 * place, 2 * (n - 1 - place) + 1)


def chunks_of(lanes):
    return -(-lanes // LANES)


def arrivals_of(n):
    return [0] + [sign * k for k in range(1, n // 2) for sign in (-1, 1)] + [n // 2]


def payload_kernel(caps, n, counts, code, first_c, second_c, mine_h, theirs, own, up, down, cols, images, own_ud, spreads, mine, sems):
    loads = fetch(((mine_h, mine),), sems)
    row, col = lax.axis_index("row"), lax.axis_index("col")
    groups, share, block = mine.shape
    cap, width = caps[0], first_c.shape[1]
    half, half2 = caps[0] // 2, caps[1] // 2
    for g in range(groups):
        cols[rows_at(g * block + (1 - col) * share, share), :] = theirs[g]
        spreads[g * cap : (g + 1) * cap, :] = picker(code[g : g + 1, :], cap)
    for way in range(2):
        stop = chunks_of(counts[way] * cap) * LANES
        own_ud[way, :, stop - LANES : stop] = jnp.zeros((cap, LANES), F32)
    pick = picker(code[pl.ds(row, 1), :], cap)
    loads[0].wait()
    for g in range(groups):
        cols[rows_at(g * block + col * share, share), :] = mine[g]
    images[...] = dot2(pick, split(cols[...]), NT)
    arrivals = arrivals_of(n)
    place = place_of(row, n)
    values = []
    for d in range(n):
        g = row_of(lax.rem(place + d, n), n)
        spread = spreads[rows_at(g * cap, cap, 16), :]
        image = images[:, pl.ds(pl.multiple_of(g * block, block), block)]
        values.append(dot2(spread, split(image), NT, flip=True))
    for d, value in enumerate(values):
        x = arrivals.index(d if d <= n // 2 else d - n)
        own[:, width + x * cap : width + (x + 1) * cap] = value
        for way, slot in ((0, (n - d) % n), (1, d)):
            if slot < counts[way]:
                own_ud[way, :, slot * cap : (slot + 1) * cap] = value
    own[:, :width] = first_c[...]
    mine_rows, mine_rows2 = rows_at(col * half, half), rows_at(col * half2, half2)
    for way, out in ((0, up), (1, down)):
        at = 0
        for c in range(width // LANES):
            out[at : at + half, :] = first_c[mine_rows, c * LANES : (c + 1) * LANES]
            at += half
        for c in range(width // LANES):
            out[at : at + half2, :] = second_c[mine_rows2, c * LANES : (c + 1) * LANES]
            at += half2
        for c in range(chunks_of(counts[way] * cap)):
            out[at : at + half, :] = own_ud[way, mine_rows, c * LANES : (c + 1) * LANES]
            at += half


def side_kernel(corner, link, cross0, diag0, link_h, link_l, link_half):
    half_width = cross0.shape[1]
    start = pl.multiple_of(lax.axis_index("col") * half_width, half_width)
    link_half[...] = link[:, pl.ds(start, half_width)]
    link_h[...], link_l[...] = split(link[...])
    value = dot3(split(corner[...]), split(link_half[...]), NN)
    cross0[...] = value
    diag0[...] = dot3((link_h[...], link_l[...]), split(value), TN)


def assemble(caps, width, flat, blk, sblk, k):
    col = lax.axis_index("col")
    half, half2 = caps[0] // 2, caps[1] // 2
    for value, side in zip(flat, (col, 1 - col)):
        rows, rows2 = rows_at(k * caps[0] + side * half, half), rows_at(k * caps[1] + side * half2, half2)
        at = 0
        for c in range(width // LANES):
            blk[rows, c * LANES : (c + 1) * LANES] = value[at : at + half, :]
            at += half
        for c in range(width // LANES):
            sblk[rows2, c * LANES : (c + 1) * LANES] = value[at : at + half2, :]
            at += half2
        for c in range((value.shape[0] - at) // half):
            blk[rows, width + c * LANES : width + (c + 1) * LANES] = value[at : at + half, :]
            at += half


def source_row(distance, n):
    return row_of(lax.rem(place_of(lax.axis_index("row"), n) + distance + n, n), n)


def factors_of(caps, n, distances, blk, sblk, code1, code2, link, lh, ll):
    cap, cap2 = caps
    width = link[0].shape[0]
    size = cap * len(distances)
    first = split(blk[:, :width])
    lh[:size, :width], ll[:size, :width] = first
    seconds = []
    for k, distance in enumerate(distances):
        g = source_row(distance, n)
        spread = dot(picker(code1[pl.ds(g, 1), :], cap), picker(code2[pl.ds(g, 1), :], cap2), NT).astype(BF16)
        seconds.append(dot2(spread, split(sblk[k * cap2 : (k + 1) * cap2, :]), NN))
    image = dot3(first, (link[0][...], link[1][...]), NN)
    for k, second in enumerate(seconds):
        rows = slice(k * cap, (k + 1) * cap)
        lh[rows, width:], ll[rows, width:] = split(second - image[rows, :])


def columns(both, half_width):
    start = lax.axis_index("col") * half_width
    f_at = pl.ds(pl.multiple_of(start, half_width), half_width)
    t_at = pl.ds(pl.multiple_of(both // 2 + start, half_width), half_width)
    return f_at, t_at


def pairs(size, values, lh, ll, rh, rl):
    both, half_width = lh.shape[1], rh.shape[1] // 2
    width = both // 2
    lh[size:, :], ll[size:, :] = split(values)
    f_at, t_at = columns(both, half_width)
    for left, right in ((lh, rh), (ll, rl)):
        for lanes, at in ((slice(0, half_width), f_at), (slice(half_width, 2 * half_width), t_at)):
            right[:size, lanes] = left[size:, at]
            right[size:, lanes] = left[:size, at]
    cross = dot3((lh[:, :width], ll[:, :width]), (rh[...], rl[...]), TN)
    close = dot3((lh[:, width:], ll[:, width:]), (rh[:, half_width:], rl[:, half_width:]), TN)
    return cross, close


def update_kernel(caps, n, k, *refs):
    arrivals = arrivals_of(n)
    fresh = k == 1
    cap = caps[0]
    (own, code1, code2, link_h, link_l), refs = refs[:5], refs[5:]
    if fresh:
        own_s, refs = refs[0], refs[1:]
    else:
        (old_v, old_ab, old_ee, old_image), refs = refs[:4], refs[4:]
    up, down = refs[:2], refs[2:4]
    v_next, ab, ee, image, blk, sblk, middle, kh, kl, lh, ll, rh, rl = refs[4:]
    both, half_width = lh.shape[1], ee.shape[1]
    width = both // 2
    news = ([0] if fresh else []) + [2 * k - 1, 2 * k]
    later = news[-1] + 1
    size = cap * len(news)
    if fresh:
        blk[:cap, :width] = own[:, :width]
        sblk[: caps[1], :] = own_s[...]
    base = len(news) - 2
    assemble(caps, width, up, blk, sblk, base)
    assemble(caps, width, down, blk, sblk, base + 1)
    factors_of(caps, n, [arrivals[x] for x in news], blk, sblk, code1, code2, (link_h, link_l), lh, ll)
    middle[...] = jnp.zeros(middle.shape, F32)
    kh[...] = jnp.zeros(kh.shape, BF16)
    kl[...] = jnp.zeros(kl.shape, BF16)
    for a, x in enumerate(news):
        rows = slice(a * cap, (a + 1) * cap)
        for y in range(x, n):
            if x == 0:
                value = own[:, width + y * cap : width + (y + 1) * cap]
            else:
                way = -1 if arrivals[x] < 0 else 1
                slot = (way * (arrivals[y] - arrivals[x])) % n
                if slot >= n - 2 * k + (1 if way < 0 or slot == 0 else 0):
                    continue
                value = blk[rows, width + slot * cap : width + (slot + 1) * cap]
            if y in news:
                b = news.index(y)
                middle[rows, b * cap : (b + 1) * cap] = value * 0.5 if y == x else value
            else:
                lanes = slice((y - later) * LANES, (y - later) * LANES + cap)
                kh[rows, lanes], kl[rows, lanes] = split(value)
    sh, sl = lh[:size, :], ll[:size, :]
    values = dot3(split(middle[...]), (sh, sl), NN)
    if not fresh:
        values = values + jnp.concatenate([old_v[:cap, :], old_v[LANES : LANES + cap, :]], axis=0)
    to_come = dot3((kh[...], kl[...]), (sh, sl), TN)
    part = split(own[:, width + news[0] * cap : width + later * cap])
    f_at, t_at = columns(both, half_width)
    image_f = dot3(part, (lh[:size, f_at], ll[:size, f_at]), NN)
    image_t = dot3(part, (lh[:size, t_at], ll[:size, t_at]), NN)
    if fresh:
        v_next[...] = to_come
        image[:, :half_width], image[:, half_width:] = image_f, image_t
    else:
        v_next[...] = old_v[2 * LANES :, :] + to_come
        image[:, :half_width] = old_image[:, :half_width] + image_f
        image[:, half_width:] = old_image[:, half_width:] + image_t
    cross, close = pairs(size, values, lh, ll, rh, rl)
    if fresh:
        ab[...], ee[...] = cross, close
    else:
        ab[...] = old_ab[...] + cross
        ee[...] = old_ee[...] + close


def last_kernel(caps, n, up, down, up_far, down_far, old_v, old_ab, old_ee, image, own, code1, code2, link_h, link_l, corner1, corner2, cross0, diag0, *refs):
    cap = caps[0]
    c1, g1, c2, xx, g2, flat, flat_far, blk, sblk, lh, ll, rh, rl, c1_v, g1_v, c2_v, xx_v, g2_v, corner1_v, corner2_v, cross0_v, diag0_v, sems = refs
    row, col = lax.axis_index("row"), lax.axis_index("col")
    both, half_width = lh.shape[1], old_ee.shape[1]
    half_at = pl.ds(pl.multiple_of(col * half_width, half_width), half_width)
    loads = [
        pltpu.make_async_copy(corner1.at[:, half_at], corner1_v, sems.at[5]),
        pltpu.make_async_copy(corner2, corner2_v, sems.at[6]),
        pltpu.make_async_copy(cross0, cross0_v, sems.at[7]),
        pltpu.make_async_copy(diag0, diag0_v, sems.at[8]),
    ]
    for load in loads:
        load.start()
    cut = up.shape[0]
    flat[:cut, :], flat[cut:, :] = up[...], down[...]
    flat_far[:cut, :], flat_far[cut:, :] = up_far[...], down_far[...]
    width = both // 2
    assemble(caps, width, (flat, flat_far), blk, sblk, 0)
    factors_of(caps, n, [n // 2], blk, sblk, code1, code2, (link_h, link_l), lh, ll)
    k = split(own[:, width + (n - 1) * cap :])
    pick = picker(code1[pl.ds(row, 1), :], cap)
    pick2 = (pick.astype(F32) * (code2[pl.ds(row, 1), :] >= 0).astype(F32)).astype(BF16)
    f_at, t_at = columns(both, half_width)
    image_f = image[:, :half_width] + dot3(k, (lh[:cap, f_at], ll[:cap, f_at]), NN)
    image_t = image[:, half_width:] + dot3(k, (lh[:cap, t_at], ll[:cap, t_at]), NN)
    values = dot3(split(blk[:, width : width + cap] * 0.5), (lh[:cap, :], ll[:cap, :]), NN) + old_v[:cap, :]
    column_f, column_t = -dot2(pick, split(image_f), TN), -dot2(pick2, split(image_t), TN)
    cross, close = pairs(cap, values, lh, ll, rh, rl)
    copies = []

    def send(value, ref, out):
        ref[...] = value
        copies.append(pltpu.make_async_copy(ref, out, sems.at[len(copies)]))
        copies[-1].start()

    send(column_f, c1_v, c1)
    send(column_t, c2_v, c2)
    for load in loads:
        load.wait()
    send(corner1_v[...] + (old_ab[:, :half_width] + cross[:, :half_width]), g1_v, g1)
    send(old_ab[:, half_width:] + cross[:, half_width:] - cross0_v[...], xx_v, xx)
    send(corner2_v[...] + (diag0_v[...] + (old_ee[...] + close)), g2_v, g2)
    for copy in copies:
        copy.wait()


def call_factors(caps, n, anc1, anc2, first_factor, second_factor):
    block, width = first_factor.shape
    codes = pltpu.VMEM((n, block), jnp.int32)
    return pl.pallas_call(
        functools.partial(factors_kernel, caps, n),
        out_shape=(
            pltpu.VMEM((caps[0], width), F32),
            pltpu.VMEM((caps[1], width), F32),
            codes,
            codes,
            pltpu.SMEM((1, 1), jnp.int32),
        ),
        in_specs=[ANY] * 4,
        out_specs=(VMEM,) * 4 + (SMEM,),
        scratch_shapes=[pltpu.VMEM(v.shape, v.dtype) for v in (anc1, anc2, first_factor, second_factor)] + [pltpu.SemaphoreType.DMA((4,))],
        cost_estimate=pl.CostEstimate(flops=8 * sum(caps) * block * width, bytes_accessed=8 * width * block, transcendentals=0),
        name="factors",
    )(anc1, anc2, first_factor, second_factor)


def call_payload(caps, n, code, first_c, second_c, mine, theirs):
    _, _, block = mine.shape
    cap, width = first_c.shape
    counts = (n - 1, n - 2)
    flats = [jax.ShapeDtypeStruct((flat_rows(caps, width, count), LANES), F32) for count in counts]
    return pl.pallas_call(
        functools.partial(payload_kernel, caps, n, counts),
        out_shape=(jax.ShapeDtypeStruct((cap, width + n * cap), F32), *flats),
        in_specs=[VMEM, VMEM, VMEM, ANY, VMEM],
        out_specs=(VMEM,) * 3,
        scratch_shapes=[
            pltpu.VMEM((n * block, block), F32),
            pltpu.VMEM((cap, n * block), F32),
            pltpu.VMEM((2, cap, chunks_of(counts[0] * cap) * LANES), F32),
            pltpu.VMEM((n * cap, block), BF16),
            pltpu.VMEM(mine.shape, F32),
            pltpu.SemaphoreType.DMA((1,)),
        ],
        cost_estimate=pl.CostEstimate(flops=8 * cap * block * n * block, bytes_accessed=8 * n * block * block, transcendentals=0),
        name="payload",
    )(code, pltpu.with_memory_space_constraint(first_c, pltpu.VMEM), second_c, mine, theirs)


def flat_rows(caps, width, count):
    return width // LANES * (caps[0] // 2 + caps[1] // 2) + chunks_of(count * caps[0]) * (caps[0] // 2)


def gather_branch(caps, n, code1, code2, second_c, own, own_up, own_down, second_link, first_corner, second_corner):
    cap = caps[0]
    block = code1.shape[1]
    width = second_link.shape[0]
    half_width = second_corner.shape[1]
    both = 2 * width
    square = jax.ShapeDtypeStruct((width, half_width), F32)
    tall = jax.ShapeDtypeStruct((block, half_width), F32)

    order = [*range(0, n, 2), *range(n - 1, 0, -2)]
    ups = [(order[k], order[(k + 1) % n]) for k in range(n)]
    downs = [(b, a) for a, b in ups]
    swap = [(0, 1), (1, 0)]

    def scratch_of(blocks):
        size = cap * blocks
        return [
            pltpu.VMEM((2 * size, both), BF16),
            pltpu.VMEM((2 * size, both), BF16),
            pltpu.VMEM((2 * size, 2 * half_width), BF16),
            pltpu.VMEM((2 * size, 2 * half_width), BF16),
        ]

    params = pltpu.CompilerParams(vmem_limit_bytes=40 << 20)
    part = pltpu.VMEM((width, width), BF16)
    cross0, diag0, link_h, link_l = pl.pallas_call(
        side_kernel,
        out_shape=(square, square, part, part),
        in_specs=[VMEM] * 2,
        out_specs=(VMEM,) * 4,
        scratch_shapes=[pltpu.VMEM((width, half_width), F32)],
        cost_estimate=pl.CostEstimate(flops=12 * width * width * half_width, bytes_accessed=20 * width * width, transcendentals=0),
        name="side",
    )(first_corner, second_link)

    up, down = own_up, own_down
    state = ()
    for k in range(1, n // 2):
        up = lax.ppermute(up[: flat_rows(caps, width, n + 1 - 2 * k)], "row", ups)
        down = lax.ppermute(down[: flat_rows(caps, width, n - 2 * k)], "row", downs)
        up_far, down_far = lax.ppermute(up, "col", swap), lax.ppermute(down, "col", swap)
        blocks = 3 if k == 1 else 2
        size = blocks * cap
        later = (n - 1 - 2 * k) * LANES
        ins = [own, code1, code2, link_h, link_l, *(state or (second_c,)), up, up_far, down, down_far]
        outs = [jax.ShapeDtypeStruct(shape, F32) for shape in ((later, both), (width, 2 * half_width), (width, half_width), (cap, 2 * half_width))]
        state = pl.pallas_call(
            functools.partial(update_kernel, caps, n, k),
            out_shape=tuple(outs),
            in_specs=[VMEM] * len(ins),
            out_specs=(VMEM,) * len(outs),
            scratch_shapes=[
                pltpu.VMEM((size, width + chunks_of((n - 1) * cap) * LANES), F32),
                pltpu.VMEM((blocks * caps[1], width), F32),
                pltpu.VMEM((size, size), F32),
                pltpu.VMEM((size, later), BF16),
                pltpu.VMEM((size, later), BF16),
            ]
            + scratch_of(blocks),
            compiler_params=params,
            cost_estimate=pl.CostEstimate(flops=6 * size * width * (2 * size + 2 * later + 6 * half_width), bytes_accessed=4 * size * width * 8, transcendentals=0),
        )(*ins)
    rows = flat_rows(caps, width, 1)
    cut = 7 * rows // 80 * 8
    k = n // 2
    up = lax.ppermute(up[:cut], "row", ups)
    down = lax.ppermute(down[cut:rows], "row", downs)
    up_far, down_far = lax.ppermute(up, "col", swap), lax.ppermute(down, "col", swap)
    return pl.pallas_call(
        functools.partial(last_kernel, caps, n),
        out_shape=(tall, square, tall, square, square),
        in_specs=[VMEM] * 13 + [ANY] * 4,
        out_specs=(ANY,) * 5,
        scratch_shapes=[pltpu.VMEM((rows, LANES), F32)] * 2
        + [pltpu.VMEM((cap, width + chunks_of(cap) * LANES), F32), pltpu.VMEM((caps[1], width), F32)]
        + scratch_of(1)
        + [pltpu.VMEM(shape.shape, F32) for shape in (tall, square, tall, square, square)]
        + [pltpu.VMEM(square.shape, F32)] * 4
        + [pltpu.SemaphoreType.DMA((9,))],
        compiler_params=params,
        cost_estimate=pl.CostEstimate(flops=6 * cap * width * (2 * width + 6 * half_width), bytes_accessed=4 * width * width * 5, transcendentals=0),
        name="last",
    )(up, down, up_far, down_far, *state, own, code1, code2, link_h, link_l, first_corner, second_corner, cross0, diag0)


def gather_plan(n, known_inverse, first_factor, first_corner, first_ancestors, second_factor, second_link, second_corner, second_ancestors):
    _, _, block = known_inverse.shape
    theirs = lax.ppermute(known_inverse, "col", [(0, 1), (1, 0)])
    anc1, anc2 = first_ancestors[None, :], second_ancestors[None, :]
    mean1, mean2 = -(-first_ancestors.shape[0] // n), -(-second_ancestors.shape[0] // n)
    caps = (min(-(-mean1 * 5 // 64) * 16, block), min(-(-mean2 * 3 // 32) * 16, block))
    first_c, second_c, code1, code2, over = call_factors(caps, n, anc1, anc2, first_factor, second_factor)
    own = call_payload(caps, n, code1, first_c, second_c, known_inverse, theirs)

    def compact(own, second_c, code1, code2, known_inverse, theirs, anc1, anc2, first_factor, second_factor, second_link, first_corner, second_corner):
        return gather_branch(caps, n, code1, code2, second_c, *own, second_link, first_corner, second_corner)

    def general(own, second_c, code1, code2, known_inverse, theirs, anc1, anc2, first_factor, second_factor, second_link, first_corner, second_corner):
        every = (block, block)
        first_c, second_c, code1, code2, _ = call_factors(every, n, anc1, anc2, first_factor, second_factor)
        own = call_payload(every, n, code1, first_c, second_c, known_inverse, theirs)
        return gather_branch(every, n, code1, code2, second_c, *own, second_link, first_corner, second_corner)

    operands = (own, second_c, code1, code2, known_inverse, theirs, anc1, anc2, first_factor, second_factor, second_link, first_corner, second_corner)
    if caps == (block, block):
        return compact(*operands)
    return lax.cond(over[0, 0] <= 0, compact, general, *operands)


def solution(mesh):
    n = mesh.shape["row"]

    def on_device(known_inverse, *rest):
        _, _, block = known_inverse.shape
        width = rest[0].shape[1]
        if n % 2 == 0 and n > 4 and block % LANES == 0 and mesh.shape["col"] == 2 and (n * block) ** 2 <= 12 * width**2:
            return gather_plan(n, known_inverse, *rest)
        return reduce_plan(known_inverse, *rest)

    return jax.shard_map(
        on_device,
        mesh=mesh,
        in_specs=(
            P("pole", "col", "row"),
            P(("pole", "row"), None),
            P("pole", None),
            P("pole"),
            P(("pole", "row"), None),
            P("pole", None),
            P("pole", "col"),
            P("pole"),
        ),
        out_specs=(
            P(("pole", "row"), "col"),
            P("pole", "col"),
            P(("pole", "row"), "col"),
            P("pole", "col"),
            P("pole", "col"),
        ),
        check_vma=False,
    )
```
